128 devices in a mesh: leaf: 16 (over z, y), front: 8 (over x, core).
Axes of the slice: x: 4, y: 4, z: 4, core: 2. Of those that a mesh axis runs over, the one named last changes fastest.
Arguments:
- right_side: bfloat16 [32, 81920], P(None, ('leaf', 'front')), may hold values from -6 to 6
- send_order: int32 [81920], P(('leaf', 'front')), may hold values from 0 to 639, as said below
- owner_order: int32 [81920], P(('leaf', 'front')), may hold values from 0 to 639, as said below
- live_rows: int32 [14], replicated, may hold values from 2048 to 4096, as said below
- lower_leaf: bfloat16 [1536, 24576], P(None, ('leaf', 'front')), may hold values from -0.109375 to 0.109375
- upper_leaf: bfloat16 [1536, 24576], P(None, ('leaf', 'front')), may hold values from -0.109375 to 0.109375
- lower_first: bfloat16 [4096, 32768], P(None, ('leaf', 'front')), may hold values from -0.0625 to 0.0625
- lower_second: bfloat16 [4096, 16384], P(None, ('leaf', 'front')), may hold values from -0.0625 to 0.0625
- lower_third: bfloat16 [4096, 8192], P(None, ('leaf', 'front')), may hold values from -0.0625 to 0.0625
- upper_first: bfloat16 [4096, 32768], P(None, ('leaf', 'front')), may hold values from -0.0625 to 0.0625
- upper_second: bfloat16 [4096, 16384], P(None, ('leaf', 'front')), may hold values from -0.0625 to 0.0625
- upper_third: bfloat16 [4096, 8192], P(None, ('leaf', 'front')), may hold values from -0.0625 to 0.0625
- downlink_first: bfloat16 [4096, 24576], P(None, ('leaf', 'front')), may hold values from -0.4375 to 0.4375
- downlink_second: bfloat16 [4096, 32768], P(None, ('leaf', 'front')), may hold values from -0.25 to 0.25
- downlink_third: bfloat16 [4096, 16384], P(None, ('leaf', 'front')), may hold values from -0.25 to 0.25
- uplink_first: bfloat16 [4096, 24576], P(None, ('leaf', 'front')), may hold values from -0.0625 to 0.0625
- uplink_second: bfloat16 [4096, 32768], P(None, ('leaf', 'front')), may hold values from -0.0625 to 0.0625
- uplink_third: bfloat16 [4096, 16384], P(None, ('leaf', 'front')), may hold values from -0.0625 to 0.0625
- pattern_first: int32 [64, 384], P(None, ('leaf', 'front')), may hold values 0 or 1
- pattern_second: int32 [64, 512], P(None, ('leaf', 'front')), may hold values 0 or 1
- pattern_third: int32 [64, 256], P(None, ('leaf', 'front')), may hold values 0 or 1
Outputs:
- solution: bfloat16 [32, 81920], P(None, ('leaf', 'front'))
The draws below stay inside these ranges and needn't reach their ends.
Inputs may be any that keep to these rules, and one draw needn't show every extreme that they name: `send_order`: each device's 640 entries are a permutation of 0 to 639. `owner_order`: each device's 640 entries are a permutation of 0 to 639. `live_rows`: multiples of 64.
All inputs are finite; a program needn't handle non-finite values. No bound on the sum of `pattern_first` or of `pattern_second` or of `pattern_third` on one device may be relied on, other than what follows from the above.
Results may differ from the reference program's by a relative error of at most 0.023.
Values may be sent and summed in bfloat16 or wider, within the bound.
No kernel may reach another device: no remote copies, remote signals or barrier semaphores. Data moves between devices by JAX's collectives and lax.ppermute only.
A program may use at most 128 MiB of HBM per device.

```python
import jax
import jax.numpy as jnp

KRYLOV = 32
SEP = 4096
LEAF_FRONT = 1536
BLOCK = 64
ROWS_DEV = 640
ROWS = 81920
NODES = 14
N_LEAF = 16
N_FRONT = 8


def device_orders(key):
    keys = jax.random.split(key, ROWS // ROWS_DEV)
    orders = jax.vmap(lambda single: jax.random.permutation(single, ROWS_DEV))(keys)
    return orders.reshape(-1).astype(jnp.int32)


def draw_send_order(key, part):
    return device_orders(jax.random.fold_in(key, 11))


def draw_owner_order(key, part):
    return device_orders(jax.random.fold_in(key, 23))


def draw_live_rows(key, part):
    first_key = jax.random.fold_in(key, 37)
    second_key = jax.random.fold_in(key, 41)
    counts = jax.random.randint(first_key, (NODES,), SEP // (2 * BLOCK), SEP // BLOCK + 1)
    chosen = jax.random.randint(second_key, (), 0, NODES)
    values = jnp.where(jnp.arange(NODES) == chosen, SEP // BLOCK, counts) * BLOCK
    return values.astype(jnp.int32)


def touch_ends(array, key, least, high):
    longest = array.shape.index(max(array.shape))
    spots = []
    for shift in (0, 1):
        where = [jax.random.randint(jax.random.fold_in(key, axis), (), 0, length) for axis, length in enumerate(array.shape)]
        where[longest] = (where[longest] + shift) % array.shape[longest]
        spots.append(tuple(where))
    return array.at[spots[0]].set(least).at[spots[1]].set(high)


def raised(values, stream_key, source, target, shards_of, factor):
    def block_of(position):
        return (jnp.arange(values.shape[position]) // (values.shape[position] // shards_of)).reshape((-1,) + (1,) * (values.ndim - 1 - position))

    one_side = jax.random.permutation(stream_key, shards_of)[block_of(target)]
    second = (block_of(target) + shards_of // 2) % shards_of
    return jnp.where((block_of(source) == one_side) | (block_of(source) == second), factor * values, values)


def steps_of(rng, extent, cuts, smallest, high):
    loudness, own = 1.0, jax.random.fold_in(rng, 6)
    for position, parts in cuts:
        heights = jnp.exp(jax.random.uniform(jax.random.fold_in(own, position), (parts,), jnp.float32, smallest / len(cuts), high / len(cuts)))
        loudness = loudness * jnp.repeat(heights, extent[position] // parts).reshape([-1 if axis == position else 1 for axis in range(len(extent))])
    return loudness


def normal_values(key, shape, scale, reach, cuts=(), held_as=jnp.bfloat16):
    drawn = jax.random.normal(key, shape, jnp.float32) * scale
    if len(cuts) > 0:
        drawn = steps_of(key, shape, cuts, -0.22, 0.18) * drawn
    return jnp.clip(drawn, min=-reach, max=reach).astype(held_as)


def bell_draw_with(key, shape, width, bound, shards, heavy, held_as=jnp.bfloat16):
    array = width * jax.random.normal(key, shape, jnp.float32)
    if shards:
        array = array * steps_of(key, shape, shards, -0.22, 0.18)
    return jnp.clip(raised(array, jax.random.fold_in(key, 3), *heavy), -bound, bound).astype(held_as)


def setup_inputs(seed: int = 0) -> dict:
    key_of = jax.random.split(jax.random.key(seed), 22)
    return {
        "right_side": normal_values(key_of[0], (KRYLOV, ROWS), 1.0, 6.0, ((1, 128),)),
        "send_order": draw_send_order(jax.random.fold_in(key_of[21], 71), 0),
        "owner_order": draw_owner_order(jax.random.fold_in(key_of[21], 71), 0),
        "live_rows": draw_live_rows(jax.random.fold_in(key_of[21], 71), 0),
        "lower_leaf": normal_values(key_of[4], (LEAF_FRONT, N_LEAF * LEAF_FRONT), (2 * LEAF_FRONT) ** -0.5, 0.109375, ((1, 128),)),
        "upper_leaf": normal_values(key_of[5], (LEAF_FRONT, N_LEAF * LEAF_FRONT), (2 * LEAF_FRONT) ** -0.5, 0.109375, ((1, 128),)),
        "lower_first": normal_values(key_of[6], (SEP, N_LEAF // 2 * SEP), (2 * SEP) ** -0.5, 0.0625, ((1, 128),)),
        "lower_second": normal_values(key_of[7], (SEP, N_LEAF // 4 * SEP), (2 * SEP) ** -0.5, 0.0625, ((1, 128),)),
        "lower_third": normal_values(key_of[8], (SEP, N_LEAF // 8 * SEP), (2 * SEP) ** -0.5, 0.0625, ((1, 128),)),
        "upper_first": normal_values(key_of[9], (SEP, N_LEAF // 2 * SEP), (2 * SEP) ** -0.5, 0.0625, ((1, 128),)),
        "upper_second": normal_values(key_of[10], (SEP, N_LEAF // 4 * SEP), (2 * SEP) ** -0.5, 0.0625, ((1, 128),)),
        "upper_third": normal_values(key_of[11], (SEP, N_LEAF // 8 * SEP), (2 * SEP) ** -0.5, 0.0625, ((1, 128),)),
        "downlink_first": bell_draw_with(key_of[12], (SEP, N_LEAF * LEAF_FRONT), (2 * LEAF_FRONT) ** -0.5, 0.4375, ((1, 128),), (1, 0, 128, 5.5)),
        "downlink_second": bell_draw_with(key_of[13], (SEP, N_LEAF // 2 * SEP), (2 * SEP) ** -0.5, 0.25, ((1, 128),), (1, 0, 128, 5.5)),
        "downlink_third": bell_draw_with(key_of[14], (SEP, N_LEAF // 4 * SEP), (2 * SEP) ** -0.5, 0.25, ((1, 128),), (1, 0, 128, 5.5)),
        "uplink_first": normal_values(key_of[15], (SEP, N_LEAF * LEAF_FRONT), (2 * SEP) ** -0.5, 0.0625, ((1, 128),)),
        "uplink_second": normal_values(key_of[16], (SEP, N_LEAF // 2 * SEP), (2 * SEP) ** -0.5, 0.0625, ((1, 128),)),
        "uplink_third": normal_values(key_of[17], (SEP, N_LEAF // 4 * SEP), (2 * SEP) ** -0.5, 0.0625, ((1, 128),)),
        "pattern_first": touch_ends((jax.random.randint(key_of[18], (SEP // BLOCK, N_LEAF * LEAF_FRONT // BLOCK), 0, 4) < 3).astype(jnp.int32), jax.random.fold_in(key_of[18], 1), 0, 1),
        "pattern_second": touch_ends((jax.random.randint(key_of[19], (SEP // BLOCK, N_LEAF // 2 * SEP // BLOCK), 0, 4) < 3).astype(jnp.int32), jax.random.fold_in(key_of[19], 1), 0, 1),
        "pattern_third": touch_ends((jax.random.randint(key_of[20], (SEP // BLOCK, N_LEAF // 4 * SEP // BLOCK), 0, 4) < 3).astype(jnp.int32), jax.random.fold_in(key_of[20], 1), 0, 1),
    }


def spread(pattern, block):
    wide = jnp.repeat(pattern, block, axis=0)
    return jnp.repeat(wide, block, axis=1).astype(jnp.bfloat16)


def reference(right_side, send_order, owner_order, live_rows, lower_leaf, upper_leaf, lower_first, lower_second, lower_third, upper_first, upper_second, upper_third, downlink_first, downlink_second, downlink_third, uplink_first, uplink_second, uplink_third, pattern_first, pattern_second, pattern_third):
    devices = N_LEAF * N_FRONT
    pair_rows = ROWS_DEV // devices
    sender = send_order.reshape(devices, ROWS_DEV)
    owner = owner_order.reshape(devices, ROWS_DEV)
    source = owner // pair_rows
    slot_in = owner % pair_rows
    target = jnp.arange(devices, dtype=jnp.int32)[:, None]
    local = sender[source, target * pair_rows + slot_in]
    anchor = (source * ROWS_DEV + local).reshape(-1).astype(jnp.int32)
    front = jnp.take(right_side, anchor, axis=1).reshape(KRYLOV, N_LEAF, N_FRONT, ROWS_DEV)
    leaf_dev = LEAF_FRONT // N_FRONT
    leaf_rhs = front[:, :, :, :leaf_dev].reshape(KRYLOV, N_LEAF, LEAF_FRONT)
    lowers = [lower_first, lower_second, lower_third]
    uppers = [upper_first, upper_second, upper_third]
    downs = [downlink_first, downlink_second, downlink_third]
    backs = [uplink_first, uplink_second, uplink_third]
    patterns = [pattern_first, pattern_second, pattern_third]
    starts = [0, N_LEAF // 2, N_LEAF // 2 + N_LEAF // 4]
    level_rhs = []
    masks = []
    offset = leaf_dev
    for level in range(1, 4):
        piece = SEP // (2 ** level * N_FRONT)
        nodes = N_LEAF // 2 ** level
        level_rhs.append(front[:, :, :, offset:offset + piece].reshape(KRYLOV, nodes, SEP))
        offset = offset + piece
        lives = live_rows[starts[level - 1]:starts[level - 1] + nodes]
        masks.append((jnp.arange(SEP, dtype=jnp.int32)[None, :] < lives[:, None]).astype(jnp.float32))
    leaf_y = []
    for group in range(N_LEAF):
        block_cols = lower_leaf[:, group * LEAF_FRONT:(group + 1) * LEAF_FRONT]
        leaf_y.append(jnp.dot(leaf_rhs[:, group], block_cols, preferred_element_type=jnp.float32).astype(jnp.bfloat16))
    children = leaf_y
    child_size = LEAF_FRONT
    level_y = []
    for level in range(1, 4):
        link = downs[level - 1] * spread(patterns[level - 1], BLOCK)
        found = []
        for node in range(N_LEAF // 2 ** level):
            total = level_rhs[level - 1][:, node].astype(jnp.float32)
            for child in (2 * node, 2 * node + 1):
                part_cols = link[:, child * child_size:(child + 1) * child_size]
                total = total - jnp.dot(children[child], part_cols.T, preferred_element_type=jnp.float32)
            mask_row = masks[level - 1][node][None, :]
            reduced = (total * mask_row).astype(jnp.bfloat16)
            solved = jnp.dot(reduced, lowers[level - 1][:, node * SEP:(node + 1) * SEP], preferred_element_type=jnp.float32)
            found.append((solved * mask_row).astype(jnp.bfloat16))
        level_y.append(found)
        children = found
        child_size = SEP
    level_x = [None, None, None]
    top = []
    for node in range(N_LEAF // 8):
        mask_row = masks[2][node][None, :]
        solved = jnp.dot(level_y[2][node], upper_third[:, node * SEP:(node + 1) * SEP], preferred_element_type=jnp.float32)
        top.append((solved * mask_row).astype(jnp.bfloat16))
    level_x[2] = top
    for level in (2, 1):
        back = backs[level] * spread(patterns[level], BLOCK)
        found = []
        for node in range(N_LEAF // 2 ** level):
            mask_row = masks[level - 1][node][None, :]
            parent = level_x[level][node // 2]
            update = level_y[level - 1][node].astype(jnp.float32) - jnp.dot(parent, back[:, node * SEP:(node + 1) * SEP], preferred_element_type=jnp.float32)
            reduced = (update * mask_row).astype(jnp.bfloat16)
            solved = jnp.dot(reduced, uppers[level - 1][:, node * SEP:(node + 1) * SEP], preferred_element_type=jnp.float32)
            found.append((solved * mask_row).astype(jnp.bfloat16))
        level_x[level - 1] = found
    back = uplink_first * spread(pattern_first, BLOCK)
    leaf_x = []
    for group in range(N_LEAF):
        parent = level_x[0][group // 2]
        update = leaf_y[group].astype(jnp.float32) - jnp.dot(parent, back[:, group * LEAF_FRONT:(group + 1) * LEAF_FRONT], preferred_element_type=jnp.float32)
        reduced = update.astype(jnp.bfloat16)
        leaf_x.append(jnp.dot(reduced, upper_leaf[:, group * LEAF_FRONT:(group + 1) * LEAF_FRONT], preferred_element_type=jnp.float32).astype(jnp.bfloat16))
    layout = [jnp.stack(leaf_x, axis=1).reshape(KRYLOV, N_LEAF, N_FRONT, leaf_dev)]
    for level in range(1, 4):
        piece = SEP // (2 ** level * N_FRONT)
        layout.append(jnp.stack(level_x[level - 1], axis=1).reshape(KRYLOV, N_LEAF, N_FRONT, piece))
    placed = jnp.concatenate(layout, axis=3).reshape(KRYLOV, ROWS)
    return jnp.zeros((KRYLOV, ROWS), jnp.bfloat16).at[:, anchor].set(placed)
```

```python
import jax
import jax.numpy as jnp
from jax import lax
from jax.sharding import Mesh, PartitionSpec as P


def spread(pattern, block):
    wide = jnp.repeat(pattern, block, axis=0)
    return jnp.repeat(wide, block, axis=1).astype(jnp.bfloat16)


GROUPS = {
    0: ("x", "c"),
    1: ("y0", "x", "c"),
    2: ("y1", "y0", "x", "c"),
    3: ("z0", "y1", "y0", "x", "c"),
}
EVERY = ("z1", "z0", "y1", "y0", "x", "c")


def collect_group(portion, level):
    axes = GROUPS[level]
    members = lax.axis_size(axes)
    copies = jnp.broadcast_to(portion[None], (members,) + portion.shape)
    gathered = lax.all_to_all(copies, axes, split_axis=0, concat_axis=0, tiled=True)
    return jnp.transpose(gathered, (1, 0, 2)).reshape(portion.shape[0], -1)


def reduce_group(term, level):
    axes = GROUPS[level]
    members = lax.axis_size(axes)
    split = jnp.transpose(term.reshape(term.shape[0], members, -1), (1, 0, 2))
    received = lax.all_to_all(split, axes, split_axis=0, concat_axis=0, tiled=True)
    return jnp.sum(received.astype(jnp.float32), axis=0)


def leaf_term(portion, matrix):
    return jnp.dot(portion, matrix, preferred_element_type=jnp.float32)


def per_device(
    right_side,
    send_order,
    owner_order,
    live_rows,
    lower_leaf,
    upper_leaf,
    lower_first,
    lower_second,
    lower_third,
    upper_first,
    upper_second,
    upper_third,
    downlink_first,
    downlink_second,
    downlink_third,
    uplink_first,
    uplink_second,
    uplink_third,
    pattern_first,
    pattern_second,
    pattern_third,
):
    fronts = lax.axis_size(("x", "c"))
    leaves = lax.axis_size(("z1", "z0", "y1", "y0"))
    place = lax.axis_index(("z1", "z0", "y1", "y0"))
    column = lax.axis_index(("x", "c"))
    columns = right_side.shape[0]
    leaf_rows = lower_leaf.shape[1]
    sep = lower_first.shape[0]
    lowers = [lower_first, lower_second, lower_third]
    uppers = [upper_first, upper_second, upper_third]
    downs = [downlink_first, downlink_second, downlink_third]
    backs = [uplink_first, uplink_second, uplink_third]
    patterns = [pattern_first, pattern_second, pattern_third]
    block = downlink_first.shape[0] // pattern_first.shape[0]
    pieces = [lower_first.shape[1], lower_second.shape[1], lower_third.shape[1]]
    starts = [0, leaves // 2, leaves // 2 + leaves // 4]
    outgoing = jnp.take(right_side, send_order, axis=1)
    arrived = lax.all_to_all(outgoing, EVERY, split_axis=1, concat_axis=1, tiled=True)
    ordered = jnp.take(arrived, owner_order, axis=1)
    leaf_rhs = ordered[:, :leaf_rows]
    level_rhs = []
    offset = leaf_rows
    for level in range(1, 4):
        level_rhs.append(ordered[:, offset : offset + pieces[level - 1]])
        offset = offset + pieces[level - 1]
    piece_masks = []
    within = []
    for level in range(1, 4):
        group = 2**level
        member = place & group - 1
        node_live = lax.dynamic_index_in_dim(
            live_rows, starts[level - 1] + (place >> level), 0, keepdims=False
        )
        first_row = (member * fronts + column) * pieces[level - 1]
        piece_masks.append(
            (first_row + jnp.arange(pieces[level - 1], dtype=jnp.int32) < node_live).astype(
                jnp.float32
            )[None, :]
        )
        within.append(member)
    expanded = [spread(patterns[index], block) for index in range(3)]
    leaf_y = leaf_term(
        collect_group(leaf_rhs, 0), matrix=lower_leaf
    ).astype(jnp.bfloat16)
    children = leaf_y
    level_y = []
    for level in range(1, 4):
        group = 2**level
        piece = pieces[level - 1]
        member = within[level - 1]
        link = downs[level - 1] * expanded[level - 1]
        term = lax.dot_general(
            children, link, (((1,), (1,)), ((), ())), preferred_element_type=jnp.float32
        ).astype(jnp.bfloat16)
        share = reduce_group(term, level)
        own_rhs = level_rhs[level - 1].astype(jnp.float32)
        reduced_piece = ((own_rhs - share) * piece_masks[level - 1]).astype(jnp.bfloat16)
        reduced_full = collect_group(reduced_piece, level)
        solved = jnp.dot(reduced_full, lowers[level - 1], preferred_element_type=jnp.float32)
        found = (solved * piece_masks[level - 1]).astype(jnp.bfloat16)
        level_y.append(found)
        children = found
    level_x = [None, None, None]
    top_full = collect_group(level_y[2], 3)
    level_x[2] = (
        jnp.dot(top_full, upper_third, preferred_element_type=jnp.float32) * piece_masks[2]
    ).astype(jnp.bfloat16)
    for level in (2, 1):
        back = backs[level] * expanded[level]
        parent_full = collect_group(level_x[level], level + 1)
        update = level_y[level - 1].astype(jnp.float32) - jnp.dot(
            parent_full, back, preferred_element_type=jnp.float32
        )
        reduced = (update * piece_masks[level - 1]).astype(jnp.bfloat16)
        reduced_full = collect_group(reduced, level)
        solved = jnp.dot(reduced_full, uppers[level - 1], preferred_element_type=jnp.float32)
        level_x[level - 1] = (solved * piece_masks[level - 1]).astype(jnp.bfloat16)
    back = uplink_first * expanded[0]
    parent_full = collect_group(level_x[0], 1)
    update = (
        leaf_y.astype(jnp.float32) - jnp.dot(parent_full, back, preferred_element_type=jnp.float32)
    ).astype(jnp.bfloat16)
    leaf_x = leaf_term(
        collect_group(update, 0), matrix=upper_leaf
    ).astype(jnp.bfloat16)
    placed = jnp.concatenate([leaf_x, level_x[0], level_x[1], level_x[2]], axis=1)
    outbound = jnp.zeros_like(placed).at[:, owner_order].set(placed)
    returned = lax.all_to_all(outbound, EVERY, split_axis=1, concat_axis=1, tiled=True)
    return jnp.zeros_like(returned).at[:, send_order].set(returned)


def solution(mesh):
    fine = Mesh(mesh.devices.reshape(2, 2, 2, 2, 4, 2), EVERY)
    by_column = P(None, EVERY)
    placed = (by_column, P(EVERY), P(EVERY), P()) + (by_column,) * 17
    return jax.shard_map(
        per_device, mesh=fine, in_specs=placed, out_specs=by_column, check_vma=False
    )
```

```python
import functools

import jax
import jax.numpy as jnp
from jax import lax
from jax.experimental import pallas as pl
from jax.experimental.pallas import tpu as pltpu
from jax.sharding import Mesh, PartitionSpec as P

EVERY = ("z1", "z0", "y1", "y0", "x", "c")
LEAVES = ("z1", "z0", "y1", "y0")
CHIPS = {
    0: ("x",),
    1: ("y0", "x"),
    2: ("y1", "y0", "x"),
    3: ("z0", "y1", "y0", "x"),
    4: ("z1", "z0", "y1", "y0", "x"),
}
MEMBERS = {0: 4, 1: 8, 2: 16, 3: 32, 4: 64}
FIRST = ("lower0", "down1")
SECOND = ("lower1", "down2", "lower2", "down3")
THIRD = ("lower3", "upper3", "back3", "upper2")
FOURTH = ("back2", "upper1", "back1", "upper0")
HALF = 16
SEP = 4096
BLOCK = 64
LEAF = 192
WIDTHS = {0: 192, 1: 256, 2: 128, 3: 64}
FIRST_NODE = {1: 0, 2: 8, 3: 12}
F32 = jnp.float32
BF16 = jnp.bfloat16
VMEM_SPEC = pl.BlockSpec(memory_space=pltpu.VMEM)
SMEM_SPEC = pl.BlockSpec(memory_space=pltpu.SMEM)


def swap(value):
    return lax.ppermute(value, "c", [(0, 1), (1, 0)])


def exchange(value, level):
    return lax.all_to_all(value, CHIPS[level], split_axis=0, concat_axis=0, tiled=True)


def call(body, name, outs, operands, live=None, scratch=()):
    scalars = () if live is None else (live,)
    return pl.pallas_call(
        body,
        name=name,
        out_shape=[jax.ShapeDtypeStruct(shape, dtype) for shape, dtype in outs],
        in_specs=[SMEM_SPEC] * len(scalars) + [VMEM_SPEC] * len(operands),
        out_specs=[VMEM_SPEC] * len(outs),
        scratch_shapes=list(scratch),
        compiler_params=pltpu.CompilerParams(vmem_limit_bytes=12 * 1024 * 1024),
    )(*scalars, *operands)


def dot(left, right):
    return jnp.dot(left, right, preferred_element_type=F32)


def lanes(shape):
    return lax.broadcasted_iota(jnp.int32, shape, len(shape) - 1)


def rows_of(shape):
    return lax.broadcasted_iota(jnp.int32, shape, 0)


def one_hot(matches):
    return jnp.where(matches, 1.0, 0.0).astype(BF16)


def dot_turned(left, right):
    return lax.dot_general(left, right, (((1,), (1,)), ((), ())), preferred_element_type=F32)


def core_index():
    return lax.axis_index("c")


def source_and_turn(order):
    source = (order * 6554) >> 15
    return source, order - source * 5


def in_order(own, other):
    core = core_index()
    first = jnp.where(core == 0, own, other)
    second = jnp.where(core == 0, other, own)
    return jnp.concatenate([first, second], axis=1)


def chip_mask(masks, level):
    start = {1: 0, 2: 512, 3: 768}[level]
    return masks[0:1, start : start + 2 * WIDTHS[level]]


def piece_masks(masks, level):
    width = WIDTHS[level]
    whole = chip_mask(masks, level)
    core = core_index()
    first = whole[:, :width]
    second = whole[:, width:]
    return jnp.where(core == 0, first, second), jnp.where(core == 0, second, first)


def pattern_rows(patterns, level):
    start = {1: 0, 2: 3, 3: 7}[level]
    count = {1: 3, 2: 4, 3: 2}[level]
    return [patterns[start + row : start + row + 1, :].astype(F32) for row in range(count)]


def pick_kernel(send_order, owner_order, right, mine, theirs):
    core = core_index()
    send = send_order[...].reshape(1, 640)
    owner = owner_order[...].reshape(1, 640)
    natural = dot(right[...], one_hot(rows_of((640, 640)) == send)).astype(BF16)
    lane = lanes((1, 1024))
    turn = lane & 7
    wanted = (((lane >> 3) & 15) * 8 + (lane >> 7)) * 5 + turn
    wanted = jnp.where(turn < 5, wanted, -1)
    picked = dot(natural, one_hot(rows_of((640, 1024)) == wanted))
    source, turn = source_and_turn(owner)
    high = jnp.broadcast_to(source[:, :256].astype(F32), (8, 256))
    low = jnp.broadcast_to(turn[:, :256].astype(F32), (8, 256))
    high_left = pltpu.roll(high, 192, 1)[:, :128]
    low_left = pltpu.roll(low, 192, 1)[:, :128]
    high_right = pltpu.roll(high, 64, 1)[:, :128]
    main_high = jnp.where(core == 0, high[:, :128], high_left)
    main_low = jnp.where(core == 0, low[:, :128], low_left)
    lane = lanes((8, 128))
    tail = jnp.where(
        core == 0,
        jnp.where(lane < 64, high[:, 128:], low_left),
        jnp.where(lane < 64, low[:, :128], high_right),
    )
    row = rows_of((8, 128))
    info = jnp.where(row == 5, main_high, 0.0)
    info = jnp.where(row == 6, main_low, info)
    info = jnp.where(row == 7, tail, info)
    tiles = []
    for half in range(2):
        part = picked[half * HALF : (half + 1) * HALF]
        stacked = jnp.concatenate([part[:, f * 128 : (f + 1) * 128] for f in range(8)], axis=0)
        tiles.append(stacked.T.reshape(16, 8, 128) + info[None])
    mine[...] = jnp.where(core == 0, tiles[0], tiles[1]).astype(BF16)
    theirs[...] = jnp.where(core == 0, tiles[1], tiles[0]).astype(BF16)


def pack_kernel(mine, other, out):
    core = core_index()
    own = mine[...].astype(F32)
    far = other[...].astype(F32)
    first = jnp.where(core == 0, own, far)
    second = jnp.where(core == 0, far, own)
    tiles = jnp.concatenate([first, second], axis=1).astype(BF16)
    for copy in range(4):
        out[:, copy] = tiles


def table_kernel(live, send_order, first, second, third, wide, masks, columns):
    hot = one_hot(lanes((BLOCK, SEP)) // BLOCK == rows_of((BLOCK, SEP)))
    start = 0
    wide[...] = jnp.zeros_like(wide)
    for pattern in (first, second, third):
        count = pattern.shape[0]
        wide[start : start + count, :] = dot(
            pattern[...].astype(F32).astype(BF16), hot
        ).astype(BF16)
        start += count
    leaf = lax.axis_index(LEAVES)
    chip = lax.axis_index("x")
    for level, start in ((1, 0), (2, 512), (3, 768)):
        width = 2 * WIDTHS[level]
        member = leaf & (2**level - 1)
        row = (member * 4 + chip) * width + lanes((8, width))
        count = live[FIRST_NODE[level] + (leaf >> level)]
        masks[:, start : start + width] = (row < count).astype(F32)
    lane = lanes((1, 1024))
    turn = lane & 7
    wanted = jnp.where(turn < 5, (lane >> 3) * 5 + turn, -1)
    hot = one_hot(rows_of((640, 1024)) == wanted)
    send = send_order[...].reshape(1, 640) + 1
    stacked = jnp.concatenate(
        [
            jnp.broadcast_to(digit.astype(F32), (8, 640))
            for digit in (send >> 3, send & 7)
        ],
        axis=0,
    )
    placed = dot(stacked.astype(BF16), hot)
    columns[...] = (placed[:8] * 8.0 + placed[8:]).astype(jnp.int32) - 1


def stack_blocks(piece, count):
    block = lanes(piece.shape) // BLOCK
    zero = jnp.zeros_like(piece)
    return jnp.concatenate(
        [jnp.where(block == index, piece, zero) for index in range(count)], axis=0
    ).astype(BF16)


def masked_sum(product, rows):
    total = None
    for index, row in enumerate(rows):
        part = product[index * HALF : (index + 1) * HALF] * row
        total = part if total is None else total + part
    return total


def store_columns(out, value):
    width = out.shape[2]
    value = value.astype(BF16)
    for index in range(out.shape[0]):
        out[index] = value[:, index * width : (index + 1) * width]


def down_product(level, pieces, links, patterns, out):
    total = None
    for piece, link, pattern in zip(pieces, links, patterns):
        rows = pattern_rows(pattern, level)
        stack = stack_blocks(piece, len(rows))
        product = dot(stack, link[...]) if level == 1 else dot_turned(stack, link[...])
        part = masked_sum(product, rows)
        total = part if total is None else total + part
    store_columns(out, total)


def apply_factor(full, factor):
    if factor.shape[0] < full.shape[1]:
        return dot_turned(full, factor[...])
    return dot(full, factor[...])


def back_product(level, full, link, pattern):
    rows = pattern_rows(pattern, level)
    stacked = jnp.concatenate([full * row for row in rows], axis=0).astype(BF16)
    product = apply_factor(stacked, link)
    block = lanes((HALF, product.shape[1])) // BLOCK
    total = product[:HALF]
    for index in range(1, len(rows)):
        part = product[index * HALF : (index + 1) * HALF]
        total = jnp.where(block == index, part, total)
    return total


def store_copies(out, value):
    value = value.astype(BF16)
    for index in range(out.shape[0]):
        out[index] = value


def joined(gathered):
    return jnp.concatenate([gathered[index] for index in range(gathered.shape[0])], axis=1)


def in_kernel(
    received, own_pattern, other_pattern, own_lower, other_lower, own_link, other_link,
    own_out, other_out, rows_out, out, turned,
):
    flat = received[...].reshape(1024, 128)
    turned[...] = flat.astype(F32).T.astype(BF16)
    info = received[pl.ds(lax.axis_index(LEAVES) * 4, 4)].astype(F32)
    rows = rows_of((1024, 128))
    lane = lanes((1, 128))
    fronts = []
    for chip in range(4):
        tile = info[chip]
        tails = (tile[7:8, :], tile[15:16, :])
        tail_high = jnp.where(lane < 64, tails[0], tails[1])
        tail_low = jnp.broadcast_to(jnp.where(lane < 64, tails[1], tails[0]), (8, 128))
        tail_low = pltpu.roll(tail_low, 64, 1)[0:1, :]
        positions = (
            tile[5:6, :] * 8.0 + tile[6:7, :],
            tail_high * 8.0 + tail_low,
            tile[13:14, :] * 8.0 + tile[14:15, :],
        )
        hot = jnp.concatenate(
            [one_hot(rows == position.astype(jnp.int32)) for position in positions], axis=1
        )
        picked = dot(turned[chip * 32 : (chip + 1) * 32, :], hot)
        fronts.append(
            jnp.where(lanes((HALF, 384)) < LEAF, picked[:HALF], picked[HALF:]).astype(BF16)
        )
    start = pl.multiple_of(lax.axis_index("x") * 32, 32)
    rows_out[...] = turned[pl.ds(start, 32), :]
    front = jnp.concatenate(fronts, axis=1)
    own = apply_factor(front, own_lower).astype(BF16)
    other = apply_factor(front, other_lower).astype(BF16)
    own_out[...] = own
    other_out[...] = other
    pieces = (own.astype(F32), other.astype(F32))
    down_product(1, pieces, (own_link, other_link), (own_pattern, other_pattern), out)


def rest_kernel(turned, own_owner, other_owner, first_out, second_out, third_out):
    core = core_index()
    parts = []
    for owner, which in ((own_owner, core), (other_owner, 1 - core)):
        source, turn = source_and_turn(owner[...].reshape(1, 640))
        hot = one_hot(rows_of((1024, 640)) == source * 8 + turn)
        rows = turned[pl.ds(pl.multiple_of(which * HALF, HALF), HALF), :]
        parts.append(dot(rows, hot))
    offset = LEAF
    for out in (first_out, second_out, third_out):
        width = out.shape[1] // 2
        own, other = (part[:, offset : offset + width] for part in parts)
        out[...] = in_order(own, other).astype(BF16)
        offset += width


def reduce_kernel(level, received, right, masks, out):
    share = received[0].astype(F32)
    for index in range(1, received.shape[0]):
        share = share + received[index].astype(F32)
    store_copies(out, (right[...].astype(F32) - share) * chip_mask(masks, level))


def solve_pieces(level, gathered, masks, own_factor, other_factor):
    full = joined(gathered)
    own_mask, other_mask = piece_masks(masks, level)
    own = (apply_factor(full, own_factor) * own_mask).astype(BF16)
    other = (apply_factor(full, other_factor) * other_mask).astype(BF16)
    return own, other


def up_kernel(
    level, gathered, masks, own_pattern, other_pattern, own_lower, other_lower, own_link,
    other_link, own_out, other_out, out,
):
    own, other = solve_pieces(level, gathered, masks, own_lower, other_lower)
    own_out[...] = own
    other_out[...] = other
    pieces = (own.astype(F32), other.astype(F32))
    links = (own_link, other_link)
    down_product(level + 1, pieces, links, (own_pattern, other_pattern), out)


def solve_kernel(level, gathered, masks, own_factor, other_factor, own_out, other_out, out):
    own, other = solve_pieces(level, gathered, masks, own_factor, other_factor)
    own_out[...] = own
    other_out[...] = other
    store_copies(out, in_order(own.astype(F32), other.astype(F32)))


def back_kernel(
    level, gathered, masks, own_pattern, other_pattern, own_y, other_y, own_link, other_link, out
):
    full = joined(gathered).astype(F32)
    own = own_y[...].astype(F32) - back_product(level + 1, full, own_link, own_pattern)
    other = other_y[...].astype(F32) - back_product(level + 1, full, other_link, other_pattern)
    if level:
        own_mask, other_mask = piece_masks(masks, level)
        own = own * own_mask
        other = other * other_mask
    store_copies(out, in_order(own, other))


def out_kernel(
    gathered, own_owner, other_owner, own_first, other_first, own_second, other_second,
    own_third, other_third, own_upper, other_upper, out,
):
    core = core_index()
    full = joined(gathered)
    tails = ((own_first, own_second, own_third), (other_first, other_second, other_third))
    placed = []
    uppers = (own_upper, other_upper)
    for which, owner in enumerate((own_owner, other_owner)):
        source, turn = source_and_turn(owner[...].reshape(1, 640))
        slot = (source & 1) * 512 + (source >> 1) * 8 + turn
        hot = one_hot(rows_of((1024, 640)) == slot)
        leaf = apply_factor(full, uppers[which])
        front = jnp.concatenate([leaf] + [tail[...].astype(F32) for tail in tails[which]], axis=1)
        total = dot_turned(front.astype(BF16), hot)
        stacked = jnp.concatenate([total[:, :512], total[:, 512:]], axis=0)
        placed.append(stacked.T.reshape(64, 8, 32))
    first = jnp.where(core == 0, placed[0], placed[1])
    second = jnp.where(core == 0, placed[1], placed[0])
    out[:, :, :32] = jnp.concatenate([first, second], axis=1).astype(BF16)
    out[:, :, 32:] = jnp.zeros((64, 16, 96), BF16)


def final_kernel(received, own_columns, other_columns, own_out, other_out):
    core = core_index()
    turned = received[...].reshape(1024, 128).astype(F32).T
    first = turned[:HALF]
    second = turned[HALF : 2 * HALF]
    own = jnp.where(core == 0, first, second).astype(BF16)
    other = jnp.where(core == 0, second, first).astype(BF16)
    work = ((own, own_columns, own_out), (other, other_columns, other_out))
    for value, columns, out in work:
        hot = one_hot(rows_of((640, 1024)) == columns[0:1, :])
        out[...] = dot_turned(value, hot).astype(BF16)


def per_device(
    right_side,
    send_order,
    owner_order,
    live_rows,
    lower_leaf,
    upper_leaf,
    lower_first,
    lower_second,
    lower_third,
    upper_first,
    upper_second,
    upper_third,
    downlink_first,
    downlink_second,
    downlink_third,
    uplink_first,
    uplink_second,
    uplink_third,
    pattern_first,
    pattern_second,
    pattern_third,
):
    core = lax.axis_index("c")
    factors = {
        "lower0": lower_leaf.T,
        "down1": downlink_first.T,
        "lower1": lower_first,
        "down2": downlink_second,
        "lower2": lower_second,
        "down3": downlink_third,
        "lower3": lower_third.T,
        "upper3": upper_third.T,
        "back3": uplink_third,
        "upper2": upper_second,
        "back2": uplink_second,
        "upper1": upper_first,
        "back1": uplink_first.T,
        "upper0": upper_leaf.T,
    }
    pairs = {}

    def begin(value, names):
        tied = lax.optimization_barrier((value,) + tuple(factors[name] for name in names))
        for name, factor in zip(names, tied[1:]):
            pairs[name] = (factors[name], swap(factor))
        return tied[0]

    def finish(value, names):
        tied = lax.optimization_barrier((value,) + tuple(pairs[name][1] for name in names))
        for name, other in zip(names, tied[1:]):
            pairs[name] = (pairs[name][0], other)
        return tied[0]

    mine, theirs = call(
        pick_kernel,
        "pick_rows",
        [((16, 8, 128), BF16)] * 2,
        (send_order, owner_order, right_side),
    )
    theirs = begin(theirs, FIRST)
    own_patterns, masks, own_columns = call(
        table_kernel,
        "tables",
        [((16, SEP), BF16), ((8, 896), F32), ((8, 1024), jnp.int32)],
        (send_order, pattern_first.T, pattern_second.T, pattern_third.T),
        live=live_rows,
    )
    other_owner = swap(owner_order)
    other_columns = swap(own_columns)
    other_patterns = swap(own_patterns)
    payload = call(
        pack_kernel, "pack_rows", [((16, 4, 16, 128), BF16)], (mine, swap(theirs))
    )[0]
    payload, masks, other_owner, other_columns, other_patterns = lax.optimization_barrier(
        (payload, masks, other_owner, other_columns, other_patterns)
    )
    patterns = (own_patterns, other_patterns)
    payload = finish(payload, FIRST)
    payload = begin(payload, SECOND)
    received = exchange(payload.reshape(64, 16, 128), 4)
    own_y, other_y, own_rows, term = call(
        in_kernel,
        "leaf_front",
        [
            ((HALF, LEAF), BF16),
            ((HALF, LEAF), BF16),
            ((32, 1024), BF16),
            ((8, HALF, 512), BF16),
        ],
        (received,) + patterns + pairs["lower0"] + pairs["down1"],
        scratch=[pltpu.VMEM((128, 1024), BF16)],
    )
    level_y = {0: (own_y, other_y)}
    rights = call(
        rest_kernel,
        "separator_rows",
        [((HALF, 512), BF16), ((HALF, 256), BF16), ((HALF, 128), BF16)],
        (own_rows, owner_order, other_owner),
    )
    for level in (1, 2, 3):
        members = MEMBERS[level]
        chip_width = SEP // members
        piece = ((HALF, WIDTHS[level]), BF16)
        if level == 1:
            term, rights = lax.optimization_barrier((term, rights))
        shared = exchange(term, level)
        reduced = call(
            functools.partial(reduce_kernel, level),
            "reduce_%d" % level,
            [((members, HALF, chip_width), BF16)],
            (shared, rights[level - 1], masks),
        )[0]
        if level == 1:
            reduced = begin(finish(reduced, SECOND), THIRD)
        elif level == 2:
            reduced = begin(finish(reduced, THIRD), FOURTH)
        else:
            reduced = finish(reduced, FOURTH)
        gathered = exchange(reduced, level)
        if level < 3:
            above = MEMBERS[level + 1]
            own_y, other_y, term = call(
                functools.partial(up_kernel, level),
                "up_%d" % level,
                [piece, piece, ((above, HALF, SEP // above), BF16)],
                (gathered, masks)
                + patterns
                + pairs["lower%d" % level]
                + pairs["down%d" % (level + 1)],
            )
        else:
            own_y, other_y, copies = call(
                functools.partial(solve_kernel, level),
                "top_lower",
                [piece, piece, ((members, HALF, chip_width), BF16)],
                (gathered, masks) + pairs["lower3"],
            )
        level_y[level] = (own_y, other_y)
    level_x = {}
    for level in (3, 2, 1):
        members = MEMBERS[level]
        chip_width = SEP // members
        piece = ((HALF, WIDTHS[level]), BF16)
        gathered = exchange(copies, level)
        own_x, other_x, copies = call(
            functools.partial(solve_kernel, level),
            "solve_%d" % level,
            [piece, piece, ((members, HALF, chip_width), BF16)],
            (gathered, masks) + pairs["upper%d" % level],
        )
        level_x[level] = (own_x, other_x)
        gathered = exchange(copies, level)
        below = level - 1
        copies = call(
            functools.partial(back_kernel, below),
            "back_%d" % below,
            [((MEMBERS[below], HALF, 2 * WIDTHS[below]), BF16)],
            (gathered, masks) + patterns + level_y[below] + pairs["back%d" % level],
        )[0]
    gathered = exchange(copies, 0)
    outbound = call(
        out_kernel,
        "leaf_solution",
        [((64, 16, 128), BF16)],
        (gathered, owner_order, other_owner)
        + level_x[1]
        + level_x[2]
        + level_x[3]
        + pairs["upper0"],
    )[0]
    returned = exchange(outbound, 4)
    own_half, other_half = call(
        final_kernel,
        "natural_order",
        [((HALF, 640), BF16), ((HALF, 640), BF16)],
        (returned, own_columns, other_columns),
    )
    far_half = swap(other_half)
    return jnp.where(
        core == 0,
        jnp.concatenate([own_half, far_half]),
        jnp.concatenate([far_half, own_half]),
    )


def solution(mesh):
    fine = Mesh(mesh.devices.reshape(2, 2, 2, 2, 4, 2), EVERY)
    by_column = P(None, EVERY)
    placed = (by_column, P(EVERY), P(EVERY), P()) + (by_column,) * 17
    return jax.shard_map(
        per_device, mesh=fine, in_specs=placed, out_specs=by_column, check_vma=False
    )
```

```python
import functools

import jax
import jax.numpy as jnp
from jax import lax
from jax.experimental import pallas as pl
from jax.experimental.pallas import tpu as pltpu
from jax.sharding import Mesh, PartitionSpec as P

EVERY = ("z1", "z0", "y1", "y0", "x", "c")
LEAVES = ("z1", "z0", "y1", "y0")
CHIPS = {
    0: ("x",),
    1: ("y0", "x"),
    2: ("y1", "y0", "x"),
    3: ("z0", "y1", "y0", "x"),
    4: ("z1", "z0", "y1", "y0", "x"),
}
MEMBERS = {0: 4, 1: 8, 2: 16, 3: 32, 4: 64}
FIRST = ("lower0", "down1", "lower1", "down2")
SECOND = ("lower2", "down3")
THIRD = ("lower3", "upper3", "back3", "upper2")
FOURTH = ("back2", "upper1", "back1", "upper0")
HALF = 16
SEP = 4096
BLOCK = 64
LEAF = 192
WIDTHS = {0: 192, 1: 256, 2: 128, 3: 64}
FIRST_NODE = {1: 0, 2: 8, 3: 12}
F32 = jnp.float32
BF16 = jnp.bfloat16
VMEM_SPEC = pl.BlockSpec(memory_space=pltpu.VMEM)
HBM_SPEC = pl.BlockSpec(memory_space=pltpu.HBM)


def swap(value):
    return lax.ppermute(value, "c", [(0, 1), (1, 0)])


def exchange(value, level):
    return lax.all_to_all(value, CHIPS[level], split_axis=0, concat_axis=0, tiled=True)


def call(body, name, outs, operands, distant=(), scratch=()):
    constrained = [pltpu.with_memory_space_constraint(value, pltpu.HBM) for value in distant]
    scratch = list(scratch)
    if distant:
        scratch.append(pltpu.SemaphoreType.DMA((len(distant),)))
    return pl.pallas_call(
        body,
        name=name,
        out_shape=[jax.ShapeDtypeStruct(shape, dtype) for shape, dtype in outs],
        in_specs=[HBM_SPEC] * len(distant) + [VMEM_SPEC] * len(operands),
        out_specs=[VMEM_SPEC] * len(outs),
        scratch_shapes=scratch,
        compiler_params=pltpu.CompilerParams(vmem_limit_bytes=12 * 1024 * 1024),
    )(*constrained, *operands)


def fetch(sources, buffers, semaphores):
    copies = [
        pltpu.make_async_copy(source, buffer, semaphores.at[index])
        for index, (source, buffer) in enumerate(zip(sources, buffers))
    ]
    for copy in copies:
        copy.start()
    return copies


def dot(left, right):
    return jnp.dot(left, right, preferred_element_type=F32)


def lanes(shape):
    return lax.broadcasted_iota(jnp.int32, shape, len(shape) - 1)


def rows_of(shape):
    return lax.broadcasted_iota(jnp.int32, shape, 0)


def one_hot(matches):
    return jnp.where(matches, 1.0, 0.0).astype(BF16)


def dot_turned(left, right):
    return lax.dot_general(left, right, (((1,), (1,)), ((), ())), preferred_element_type=F32)


def core_index():
    return lax.axis_index("c")


def source_and_turn(order):
    source = (order * 6554) >> 15
    return source, order - source * 5


def in_order(own, other):
    core = core_index()
    first = jnp.where(core == 0, own, other)
    second = jnp.where(core == 0, other, own)
    return jnp.concatenate([first, second], axis=1)


def chip_mask(masks, level):
    start = {1: 0, 2: 512, 3: 768}[level]
    return masks[0:1, start : start + 2 * WIDTHS[level]]


def piece_masks(masks, level):
    width = WIDTHS[level]
    whole = chip_mask(masks, level)
    core = core_index()
    first = whole[:, :width]
    second = whole[:, width:]
    return jnp.where(core == 0, first, second), jnp.where(core == 0, second, first)


def pattern_rows(patterns, level):
    start = {1: 0, 2: 3, 3: 7}[level]
    count = {1: 3, 2: 4, 3: 2}[level]
    return [patterns[start + row : start + row + 1, :].astype(F32) for row in range(count)]


def pick_rows(send_order, owner_order, right, mine, theirs):
    core = core_index()
    send = send_order[...].reshape(1, 640)
    owner = owner_order[...].reshape(1, 640)
    natural = dot(right[...], one_hot(rows_of((640, 640)) == send)).astype(BF16)
    lane = lanes((1, 1024))
    turn = lane & 7
    wanted = (((lane >> 3) & 15) * 8 + (lane >> 7)) * 5 + turn
    wanted = jnp.where(turn < 5, wanted, -1)
    picked = dot(natural, one_hot(rows_of((640, 1024)) == wanted))
    source, turn = source_and_turn(owner)
    high = jnp.broadcast_to(source[:, :256].astype(F32), (8, 256))
    low = jnp.broadcast_to(turn[:, :256].astype(F32), (8, 256))
    high_left = pltpu.roll(high, 192, 1)[:, :128]
    low_left = pltpu.roll(low, 192, 1)[:, :128]
    high_right = pltpu.roll(high, 64, 1)[:, :128]
    main_high = jnp.where(core == 0, high[:, :128], high_left)
    main_low = jnp.where(core == 0, low[:, :128], low_left)
    lane = lanes((8, 128))
    tail = jnp.where(
        core == 0,
        jnp.where(lane < 64, high[:, 128:], low_left),
        jnp.where(lane < 64, low[:, :128], high_right),
    )
    row = rows_of((8, 128))
    info = jnp.where(row == 5, main_high, 0.0)
    info = jnp.where(row == 6, main_low, info)
    info = jnp.where(row == 7, tail, info)
    tiles = []
    for half in range(2):
        part = picked[half * HALF : (half + 1) * HALF]
        stacked = jnp.concatenate([part[:, f * 128 : (f + 1) * 128] for f in range(8)], axis=0)
        tiles.append(stacked.T.reshape(16, 8, 128) + info[None])
    mine[...] = jnp.where(core == 0, tiles[0], tiles[1]).astype(BF16)
    theirs[...] = jnp.where(core == 0, tiles[1], tiles[0]).astype(BF16)


def pack_kernel(mine, other, out):
    core = core_index()
    own = mine[...].astype(F32)
    far = other[...].astype(F32)
    first = jnp.where(core == 0, own, far)
    second = jnp.where(core == 0, far, own)
    tiles = jnp.concatenate([first, second], axis=1).astype(BF16)
    for copy in range(4):
        out[:, copy] = tiles


def make_tables(live, send_order, owner_order, first, second, third, wide, masks, columns):
    hot = one_hot(lanes((BLOCK, SEP)) // BLOCK == rows_of((BLOCK, SEP)))
    start = 0
    wide[...] = jnp.zeros_like(wide)
    for pattern in (first, second, third):
        count = pattern.shape[0]
        wide[start : start + count, :] = dot(
            pattern[...].astype(F32).astype(BF16), hot
        ).astype(BF16)
        start += count
    leaf = lax.axis_index(LEAVES)
    chip = lax.axis_index("x")
    for level, start in ((1, 0), (2, 512), (3, 768)):
        width = 2 * WIDTHS[level]
        member = leaf & (2**level - 1)
        row = (member * 4 + chip) * width + lanes((8, width))
        count = live[FIRST_NODE[level] + (leaf >> level)]
        masks[:, start : start + width] = (row < count).astype(F32)
    lane = lanes((1, 1024))
    turn = lane & 7
    device = ((lane >> 3) & 63) * 2 + (lane >> 9)
    wanted = jnp.where(turn < 5, device * 5 + turn, -1)
    hot = one_hot(rows_of((640, 1024)) == wanted)
    send = send_order[...].reshape(1, 640) + 1
    stacked = jnp.concatenate(
        [
            jnp.broadcast_to(digit.astype(F32), (8, 640))
            for digit in (send >> 3, send & 7)
        ],
        axis=0,
    )
    placed = dot(stacked.astype(BF16), hot)
    row = rows_of((8, 1024))
    owner = jnp.broadcast_to(owner_order[...].reshape(1, 640), (8, 640))
    owner = jnp.concatenate([owner, jnp.zeros((8, 384), jnp.int32)], axis=1)
    values = (placed[:8] * 8.0 + placed[8:]).astype(jnp.int32) - 1
    columns[...] = jnp.where(row == 0, values, owner)


def start_kernel(
    live, send_order, owner_order, right, first, second, third, mine, theirs, wide, masks,
    columns, live_buffer, send_buffer, owner_buffer, right_buffer, first_buffer, second_buffer,
    third_buffer, semaphores,
):
    buffers = (
        live_buffer, send_buffer, owner_buffer, right_buffer, first_buffer, second_buffer,
        third_buffer,
    )
    sources = (live, send_order, owner_order, right, first, second, third)
    for copy in fetch(sources, buffers, semaphores):
        copy.wait()
    pick_rows(send_buffer, owner_buffer, right_buffer, mine, theirs)
    make_tables(
        live_buffer, send_buffer, owner_buffer, first_buffer, second_buffer, third_buffer, wide,
        masks, columns,
    )


def stack_blocks(piece, count):
    block = lanes(piece.shape) // BLOCK
    zero = jnp.zeros_like(piece)
    return jnp.concatenate(
        [jnp.where(block == index, piece, zero) for index in range(count)], axis=0
    ).astype(BF16)


def masked_sum(product, rows):
    total = None
    for index, row in enumerate(rows):
        part = product[index * HALF : (index + 1) * HALF] * row
        total = part if total is None else total + part
    return total


def store_columns(out, value):
    width = out.shape[2]
    value = value.astype(BF16)
    for index in range(out.shape[0]):
        out[index] = value[:, index * width : (index + 1) * width]


def down_product(level, pieces, links, patterns, out):
    total = None
    for piece, link, pattern in zip(pieces, links, patterns):
        rows = pattern_rows(pattern, level)
        stack = stack_blocks(piece, len(rows))
        product = dot(stack, link[...]) if level == 1 else dot_turned(stack, link[...])
        part = masked_sum(product, rows)
        total = part if total is None else total + part
    store_columns(out, total)


def apply_factor(full, factor):
    if factor.shape[0] < full.shape[1]:
        return dot_turned(full, factor[...])
    return dot(full, factor[...])


def back_product(level, full, link, pattern):
    rows = pattern_rows(pattern, level)
    stacked = jnp.concatenate([full * row for row in rows], axis=0).astype(BF16)
    product = apply_factor(stacked, link)
    block = lanes((HALF, product.shape[1])) // BLOCK
    total = product[:HALF]
    for index in range(1, len(rows)):
        part = product[index * HALF : (index + 1) * HALF]
        total = jnp.where(block == index, part, total)
    return total


def store_copies(out, value):
    value = value.astype(BF16)
    for index in range(out.shape[0]):
        out[index] = value


def joined(gathered):
    return jnp.concatenate([gathered[index] for index in range(gathered.shape[0])], axis=1)


def in_kernel(
    far_lower, far_link, received, own_pattern, other_pattern, other_lower, other_link,
    own_out, other_out, rows_out, out, turned, own_lower, own_link, semaphores,
):
    copies = fetch((far_lower, far_link), (own_lower, own_link), semaphores)
    flat = received[...].reshape(1024, 128)
    turned[...] = flat.astype(F32).T.astype(BF16)
    info = received[pl.ds(lax.axis_index(LEAVES) * 4, 4)].astype(F32)
    rows = rows_of((1024, 128))
    lane = lanes((1, 128))
    fronts = []
    for chip in range(4):
        tile = info[chip]
        tails = (tile[7:8, :], tile[15:16, :])
        tail_high = jnp.where(lane < 64, tails[0], tails[1])
        tail_low = jnp.broadcast_to(jnp.where(lane < 64, tails[1], tails[0]), (8, 128))
        tail_low = pltpu.roll(tail_low, 64, 1)[0:1, :]
        positions = (
            tile[5:6, :] * 8.0 + tile[6:7, :],
            tail_high * 8.0 + tail_low,
            tile[13:14, :] * 8.0 + tile[14:15, :],
        )
        hot = jnp.concatenate(
            [one_hot(rows == position.astype(jnp.int32)) for position in positions], axis=1
        )
        picked = dot(turned[chip * 32 : (chip + 1) * 32, :], hot)
        fronts.append(
            jnp.where(lanes((HALF, 384)) < LEAF, picked[:HALF], picked[HALF:]).astype(BF16)
        )
    start = pl.multiple_of(lax.axis_index("x") * 32, 32)
    rows_out[...] = turned[pl.ds(start, 32), :]
    front = jnp.concatenate(fronts, axis=1)
    copies[0].wait()
    own = apply_factor(front, own_lower).astype(BF16)
    other = apply_factor(front, other_lower).astype(BF16)
    own_out[...] = own
    other_out[...] = other
    pieces = (own.astype(F32), other.astype(F32))
    copies[1].wait()
    down_product(1, pieces, (own_link, other_link), (own_pattern, other_pattern), out)


def rest_kernel(turned, own_owner, other_owner, first_out, second_out, third_out):
    core = core_index()
    parts = []
    for owner, which in ((own_owner, core), (other_owner, 1 - core)):
        source, turn = source_and_turn(owner[1:2, :640])
        hot = one_hot(rows_of((1024, 640)) == source * 8 + turn)
        rows = turned[pl.ds(pl.multiple_of(which * HALF, HALF), HALF), :]
        parts.append(dot(rows, hot))
    offset = LEAF
    for out in (first_out, second_out, third_out):
        width = out.shape[1] // 2
        own, other = (part[:, offset : offset + width] for part in parts)
        out[...] = in_order(own, other).astype(BF16)
        offset += width


def reduce_kernel(level, received, right, masks, out):
    share = received[0].astype(F32)
    for index in range(1, received.shape[0]):
        share = share + received[index].astype(F32)
    store_copies(out, (right[...].astype(F32) - share) * chip_mask(masks, level))


def solve_pieces(level, gathered, masks, own_factor, other_factor):
    full = joined(gathered)
    own_mask, other_mask = piece_masks(masks, level)
    own = (apply_factor(full, own_factor) * own_mask).astype(BF16)
    other = (apply_factor(full, other_factor) * other_mask).astype(BF16)
    return own, other


def up_kernel(
    level, gathered, masks, own_pattern, other_pattern, own_lower, other_lower, own_link,
    other_link, own_out, other_out, out,
):
    own, other = solve_pieces(level, gathered, masks, own_lower, other_lower)
    own_out[...] = own
    other_out[...] = other
    pieces = (own.astype(F32), other.astype(F32))
    links = (own_link, other_link)
    down_product(level + 1, pieces, links, (own_pattern, other_pattern), out)


def solve_kernel(level, gathered, masks, own_factor, other_factor, own_out, other_out, out):
    own, other = solve_pieces(level, gathered, masks, own_factor, other_factor)
    own_out[...] = own
    other_out[...] = other
    store_copies(out, in_order(own.astype(F32), other.astype(F32)))


def back_kernel(
    level, gathered, masks, own_pattern, other_pattern, own_y, other_y, own_link, other_link, out
):
    full = joined(gathered).astype(F32)
    own = own_y[...].astype(F32) - back_product(level + 1, full, own_link, own_pattern)
    other = other_y[...].astype(F32) - back_product(level + 1, full, other_link, other_pattern)
    if level:
        own_mask, other_mask = piece_masks(masks, level)
        own = own * own_mask
        other = other * other_mask
    store_copies(out, in_order(own, other))


def out_kernel(
    gathered, own_owner, other_owner, own_first, other_first, own_second, other_second,
    own_third, other_third, own_upper, other_upper, out,
):
    core = core_index()
    full = joined(gathered)
    tails = ((own_first, own_second, own_third), (other_first, other_second, other_third))
    placed = []
    uppers = (own_upper, other_upper)
    for which, owner in enumerate((own_owner, other_owner)):
        source, turn = source_and_turn(owner[1:2, :640])
        slot = (source & 1) * 512 + (source >> 1) * 8 + turn
        hot = one_hot(rows_of((1024, 640)) == slot)
        leaf = apply_factor(full, uppers[which])
        front = jnp.concatenate([leaf] + [tail[...].astype(F32) for tail in tails[which]], axis=1)
        total = dot_turned(front.astype(BF16), hot)
        placed.append(jnp.concatenate([total[:, :512], total[:, 512:]], axis=0))
    first = jnp.where(core == 0, placed[0], placed[1])
    second = jnp.where(core == 0, placed[1], placed[0])
    unused = jnp.zeros((64, 512), F32)
    stacked = jnp.concatenate([first, second, unused], axis=0)
    out[...] = stacked.T.reshape(64, 8, 128).astype(BF16)


def final_kernel(received, own_columns, other_columns, own_out, other_out):
    core = core_index()
    turned = received[...].reshape(512, 128).astype(F32).T
    first = jnp.concatenate([turned[:HALF], turned[2 * HALF : 3 * HALF]], axis=1)
    second = jnp.concatenate([turned[HALF : 2 * HALF], turned[3 * HALF : 4 * HALF]], axis=1)
    own = jnp.where(core == 0, first, second).astype(BF16)
    other = jnp.where(core == 0, second, first).astype(BF16)
    work = ((own, own_columns, own_out), (other, other_columns, other_out))
    for value, columns, out in work:
        hot = one_hot(rows_of((640, 1024)) == columns[0:1, :])
        out[...] = dot_turned(value, hot).astype(BF16)


def per_device(
    right_side,
    send_order,
    owner_order,
    live_rows,
    lower_leaf,
    upper_leaf,
    lower_first,
    lower_second,
    lower_third,
    upper_first,
    upper_second,
    upper_third,
    downlink_first,
    downlink_second,
    downlink_third,
    uplink_first,
    uplink_second,
    uplink_third,
    pattern_first,
    pattern_second,
    pattern_third,
):
    core = lax.axis_index("c")
    factors = {
        "lower0": lower_leaf.T,
        "down1": downlink_first.T,
        "lower1": lower_first,
        "down2": downlink_second,
        "lower2": lower_second,
        "down3": downlink_third,
        "lower3": lower_third.T,
        "upper3": upper_third.T,
        "back3": uplink_third,
        "upper2": upper_second,
        "back2": uplink_second,
        "upper1": upper_first,
        "back1": uplink_first.T,
        "upper0": upper_leaf.T,
    }
    pairs = {}

    def begin(value, names):
        tied = lax.optimization_barrier((value,) + tuple(factors[name] for name in names))
        for name, factor in zip(names, tied[1:]):
            pairs[name] = (factors[name], swap(factor))
        return tied[0]

    def finish(value, names):
        tied = lax.optimization_barrier((value,) + tuple(pairs[name][1] for name in names))
        for name, other in zip(names, tied[1:]):
            pairs[name] = (pairs[name][0], other)
        return tied[0]

    mine, theirs, own_patterns, masks, own_columns = call(
        start_kernel,
        "start",
        [
            ((16, 8, 128), BF16),
            ((16, 8, 128), BF16),
            ((16, SEP), BF16),
            ((8, 896), F32),
            ((8, 1024), jnp.int32),
        ],
        (),
        distant=(
            live_rows,
            send_order,
            owner_order,
            right_side,
            pattern_first.T,
            pattern_second.T,
            pattern_third.T,
        ),
        scratch=[
            pltpu.SMEM((14,), jnp.int32),
            pltpu.VMEM((640,), jnp.int32),
            pltpu.VMEM((640,), jnp.int32),
            pltpu.VMEM((32, 640), BF16),
            pltpu.VMEM((3, BLOCK), jnp.int32),
            pltpu.VMEM((4, BLOCK), jnp.int32),
            pltpu.VMEM((2, BLOCK), jnp.int32),
        ],
    )
    other_columns = swap(own_columns)
    other_patterns = swap(own_patterns)
    payload = call(
        pack_kernel, "pack_rows", [((16, 4, 16, 128), BF16)], (mine, swap(theirs))
    )[0]
    payload, other_columns, other_patterns = lax.optimization_barrier(
        (payload, other_columns, other_patterns)
    )
    patterns = (own_patterns, other_patterns)
    payload = begin(payload, FIRST)
    received = finish(exchange(payload.reshape(64, 16, 128), 4), FIRST)
    own_y, other_y, own_rows, term = call(
        in_kernel,
        "leaf_front",
        [
            ((HALF, LEAF), BF16),
            ((HALF, LEAF), BF16),
            ((32, 1024), BF16),
            ((8, HALF, 512), BF16),
        ],
        (received,) + patterns + (pairs["lower0"][1], pairs["down1"][1]),
        distant=(pairs["lower0"][0], pairs["down1"][0]),
        scratch=[
            pltpu.VMEM((128, 1024), BF16),
            pltpu.VMEM((LEAF, 8 * LEAF), BF16),
            pltpu.VMEM((LEAF, SEP), BF16),
        ],
    )
    level_y = {0: (own_y, other_y)}
    rights = call(
        rest_kernel,
        "separator_rows",
        [((HALF, 512), BF16), ((HALF, 256), BF16), ((HALF, 128), BF16)],
        (own_rows, own_columns, other_columns),
    )
    for level in (1, 2, 3):
        members = MEMBERS[level]
        chip_width = SEP // members
        piece = ((HALF, WIDTHS[level]), BF16)
        if level == 1:
            term, rights = lax.optimization_barrier((term, rights))
            term = begin(term, SECOND)
        shared = exchange(term, level)
        reduced = call(
            functools.partial(reduce_kernel, level),
            "reduce_%d" % level,
            [((members, HALF, chip_width), BF16)],
            (shared, rights[level - 1], masks),
        )[0]
        if level == 1:
            reduced = begin(finish(reduced, SECOND), THIRD)
        elif level == 2:
            reduced = begin(finish(reduced, THIRD), FOURTH)
        else:
            reduced = finish(reduced, FOURTH)
        gathered = exchange(reduced, level)
        if level < 3:
            above = MEMBERS[level + 1]
            own_y, other_y, term = call(
                functools.partial(up_kernel, level),
                "up_%d" % level,
                [piece, piece, ((above, HALF, SEP // above), BF16)],
                (gathered, masks)
                + patterns
                + pairs["lower%d" % level]
                + pairs["down%d" % (level + 1)],
            )
        else:
            own_y, other_y, copies = call(
                functools.partial(solve_kernel, level),
                "top_lower",
                [piece, piece, ((members, HALF, chip_width), BF16)],
                (gathered, masks) + pairs["lower3"],
            )
        level_y[level] = (own_y, other_y)
    level_x = {}
    for level in (3, 2, 1):
        members = MEMBERS[level]
        chip_width = SEP // members
        piece = ((HALF, WIDTHS[level]), BF16)
        gathered = exchange(copies, level)
        own_x, other_x, copies = call(
            functools.partial(solve_kernel, level),
            "solve_%d" % level,
            [piece, piece, ((members, HALF, chip_width), BF16)],
            (gathered, masks) + pairs["upper%d" % level],
        )
        level_x[level] = (own_x, other_x)
        gathered = exchange(copies, level)
        below = level - 1
        copies = call(
            functools.partial(back_kernel, below),
            "back_%d" % below,
            [((MEMBERS[below], HALF, 2 * WIDTHS[below]), BF16)],
            (gathered, masks) + patterns + level_y[below] + pairs["back%d" % level],
        )[0]
    gathered = exchange(copies, 0)
    outbound = call(
        out_kernel,
        "leaf_solution",
        [((64, 8, 128), BF16)],
        (gathered, own_columns, other_columns)
        + level_x[1]
        + level_x[2]
        + level_x[3]
        + pairs["upper0"],
    )[0]
    returned = exchange(outbound, 4)
    own_half, other_half = call(
        final_kernel,
        "natural_order",
        [((HALF, 640), BF16), ((HALF, 640), BF16)],
        (returned, own_columns, other_columns),
    )
    far_half = swap(other_half)
    return jnp.where(
        core == 0,
        jnp.concatenate([own_half, far_half]),
        jnp.concatenate([far_half, own_half]),
    )


def solution(mesh):
    fine = Mesh(mesh.devices.reshape(2, 2, 2, 2, 4, 2), EVERY)
    by_column = P(None, EVERY)
    placed = (by_column, P(EVERY), P(EVERY), P()) + (by_column,) * 17
    return jax.shard_map(
        per_device, mesh=fine, in_specs=placed, out_specs=by_column, check_vma=False
    )
```

```python
import functools

import jax
import jax.numpy as jnp
from jax import lax
from jax.experimental import pallas as pl
from jax.experimental.pallas import tpu as pltpu
from jax.sharding import Mesh, PartitionSpec as P

EVERY = ("z1", "z0", "y1", "y0", "x", "c")
LEAVES = ("z1", "z0", "y1", "y0")
CHIPS = {
    0: ("x",),
    1: ("y0", "x"),
    2: ("y1", "y0", "x"),
    3: ("z0", "y1", "y0", "x"),
    4: ("z1", "z0", "y1", "y0", "x"),
}
MEMBERS = {0: 4, 1: 8, 2: 16, 3: 32, 4: 64}
FIRST = ("lower0", "down1", "lower1", "down2")
SECOND = ("lower2", "down3")
THIRD = ("lower3", "upper3", "back3", "upper2")
FOURTH = ("back2", "upper1", "back1", "upper0")
HALF = 16
SEP = 4096
BLOCK = 64
LEAF = 192
WIDTHS = {0: 192, 1: 256, 2: 128, 3: 64}
FIRST_NODE = {1: 0, 2: 8, 3: 12}
F32 = jnp.float32
BF16 = jnp.bfloat16
VMEM_SPEC = pl.BlockSpec(memory_space=pltpu.VMEM)
HBM_SPEC = pl.BlockSpec(memory_space=pltpu.HBM)


def swap(value):
    return lax.ppermute(value, "c", [(0, 1), (1, 0)])


def exchange(value, level):
    return lax.all_to_all(value, CHIPS[level], split_axis=0, concat_axis=0, tiled=True)


def call(body, name, outs, operands, distant=(), scratch=()):
    constrained = [pltpu.with_memory_space_constraint(value, pltpu.HBM) for value in distant]
    scratch = list(scratch)
    if distant:
        scratch.append(pltpu.SemaphoreType.DMA((len(distant),)))
    return pl.pallas_call(
        body,
        name=name,
        out_shape=[jax.ShapeDtypeStruct(shape, dtype) for shape, dtype in outs],
        in_specs=[HBM_SPEC] * len(distant) + [VMEM_SPEC] * len(operands),
        out_specs=[VMEM_SPEC] * len(outs),
        scratch_shapes=scratch,
        compiler_params=pltpu.CompilerParams(vmem_limit_bytes=12 * 1024 * 1024),
    )(*constrained, *operands)


def fetch(sources, buffers, semaphores):
    copies = [
        pltpu.make_async_copy(source, buffer, semaphores.at[index])
        for index, (source, buffer) in enumerate(zip(sources, buffers))
    ]
    for copy in copies:
        copy.start()
    return copies


def dot(left, right):
    return jnp.dot(left, right, preferred_element_type=F32)


def lanes(shape):
    return lax.broadcasted_iota(jnp.int32, shape, len(shape) - 1)


def rows_of(shape):
    return lax.broadcasted_iota(jnp.int32, shape, 0)


def one_hot(matches):
    return jnp.where(matches, 1.0, 0.0).astype(BF16)


def dot_turned(left, right):
    return lax.dot_general(left, right, (((1,), (1,)), ((), ())), preferred_element_type=F32)


def core_index():
    return lax.axis_index("c")


def source_and_turn(order):
    source = (order * 6554) >> 15
    return source, order - source * 5


def in_order(own, other):
    core = core_index()
    first = jnp.where(core == 0, own, other)
    second = jnp.where(core == 0, other, own)
    return jnp.concatenate([first, second], axis=1)


def chip_mask(masks, level):
    start = {1: 0, 2: 512, 3: 768}[level]
    return masks[0:1, start : start + 2 * WIDTHS[level]]


def piece_masks(masks, level):
    width = WIDTHS[level]
    whole = chip_mask(masks, level)
    core = core_index()
    first = whole[:, :width]
    second = whole[:, width:]
    return jnp.where(core == 0, first, second), jnp.where(core == 0, second, first)


def pattern_rows(patterns, level):
    start = {1: 0, 2: 3, 3: 7}[level]
    count = {1: 3, 2: 4, 3: 2}[level]
    return [patterns[start + row : start + row + 1, :].astype(F32) for row in range(count)]


def pick_rows(send_order, owner_order, right, mine, theirs):
    core = core_index()
    send = send_order[...].reshape(1, 640)
    owner = owner_order[...].reshape(1, 640)
    natural = dot(right[...], one_hot(rows_of((640, 640)) == send)).astype(BF16)
    lane = lanes((1, 1024))
    turn = lane & 7
    wanted = (((lane >> 3) & 15) * 8 + (lane >> 7)) * 5 + turn
    wanted = jnp.where(turn < 5, wanted, -1)
    picked = dot(natural, one_hot(rows_of((640, 1024)) == wanted))
    source, turn = source_and_turn(owner)
    high = jnp.broadcast_to(source[:, :256].astype(F32), (8, 256))
    low = jnp.broadcast_to(turn[:, :256].astype(F32), (8, 256))
    high_left = pltpu.roll(high, 192, 1)[:, :128]
    low_left = pltpu.roll(low, 192, 1)[:, :128]
    high_right = pltpu.roll(high, 64, 1)[:, :128]
    main_high = jnp.where(core == 0, high[:, :128], high_left)
    main_low = jnp.where(core == 0, low[:, :128], low_left)
    lane = lanes((8, 128))
    tail = jnp.where(
        core == 0,
        jnp.where(lane < 64, high[:, 128:], low_left),
        jnp.where(lane < 64, low[:, :128], high_right),
    )
    row = rows_of((8, 128))
    info = jnp.where(row == 5, main_high, 0.0)
    info = jnp.where(row == 6, main_low, info)
    info = jnp.where(row == 7, tail, info)
    tiles = []
    for half in range(2):
        part = picked[half * HALF : (half + 1) * HALF]
        stacked = jnp.concatenate([part[:, f * 128 : (f + 1) * 128] for f in range(8)], axis=0)
        tiles.append(stacked.T.reshape(16, 8, 128) + info[None])
    mine[...] = jnp.where(core == 0, tiles[0], tiles[1]).astype(BF16)
    theirs[...] = jnp.where(core == 0, tiles[1], tiles[0]).astype(BF16)


def pack_kernel(mine, other, out):
    core = core_index()
    own = mine[...].astype(F32)
    far = other[...].astype(F32)
    first = jnp.where(core == 0, own, far)
    second = jnp.where(core == 0, far, own)
    tiles = jnp.concatenate([first, second], axis=1).astype(BF16)
    for copy in range(4):
        out[:, copy] = tiles


def make_tables(live, send_order, owner_order, first, second, third, wide, masks, columns):
    hot = one_hot(lanes((BLOCK, SEP)) // BLOCK == rows_of((BLOCK, SEP)))
    start = 0
    wide[...] = jnp.zeros_like(wide)
    for pattern in (first, second, third):
        count = pattern.shape[0]
        wide[start : start + count, :] = dot(
            pattern[...].astype(F32).astype(BF16), hot
        ).astype(BF16)
        start += count
    leaf = lax.axis_index(LEAVES)
    chip = lax.axis_index("x")
    for level, start in ((1, 0), (2, 512), (3, 768)):
        width = 2 * WIDTHS[level]
        member = leaf & (2**level - 1)
        row = (member * 4 + chip) * width + lanes((8, width))
        count = live[FIRST_NODE[level] + (leaf >> level)]
        masks[:, start : start + width] = (row < count).astype(F32)
    lane = lanes((1, 1024))
    turn = lane & 7
    device = ((lane >> 3) & 63) * 2 + (lane >> 9)
    wanted = jnp.where(turn < 5, device * 5 + turn, -1)
    hot = one_hot(rows_of((640, 1024)) == wanted)
    send = send_order[...].reshape(1, 640) + 1
    stacked = jnp.concatenate(
        [
            jnp.broadcast_to(digit.astype(F32), (8, 640))
            for digit in (send >> 3, send & 7)
        ],
        axis=0,
    )
    placed = dot(stacked.astype(BF16), hot)
    row = rows_of((8, 1024))
    owner = jnp.broadcast_to(owner_order[...].reshape(1, 640), (8, 640))
    owner = jnp.concatenate([owner, jnp.zeros((8, 384), jnp.int32)], axis=1)
    values = (placed[:8] * 8.0 + placed[8:]).astype(jnp.int32) - 1
    columns[...] = jnp.where(row == 0, values, owner)


def start_kernel(
    live, send_order, owner_order, right, first, second, third, lower, link, mine, theirs, wide,
    masks, columns, lower_out, link_out, live_buffer, send_buffer, owner_buffer, right_buffer,
    first_buffer, second_buffer, third_buffer, semaphores,
):
    buffers = (
        live_buffer, send_buffer, owner_buffer, right_buffer, first_buffer, second_buffer,
        third_buffer, lower_out, link_out,
    )
    sources = (live, send_order, owner_order, right, first, second, third, lower, link)
    copies = fetch(sources, buffers, semaphores)
    for copy in copies[:7]:
        copy.wait()
    pick_rows(send_buffer, owner_buffer, right_buffer, mine, theirs)
    make_tables(
        live_buffer, send_buffer, owner_buffer, first_buffer, second_buffer, third_buffer, wide,
        masks, columns,
    )
    for copy in copies[7:]:
        copy.wait()


def stack_blocks(piece, count):
    block = lanes(piece.shape) // BLOCK
    zero = jnp.zeros_like(piece)
    return jnp.concatenate(
        [jnp.where(block == index, piece, zero) for index in range(count)], axis=0
    ).astype(BF16)


def masked_sum(product, rows):
    total = None
    for index, row in enumerate(rows):
        part = product[index * HALF : (index + 1) * HALF] * row
        total = part if total is None else total + part
    return total


def store_columns(out, value):
    width = out.shape[2]
    value = value.astype(BF16)
    for index in range(out.shape[0]):
        out[index] = value[:, index * width : (index + 1) * width]


def down_product(level, pieces, links, patterns, out):
    total = None
    for piece, link, pattern in zip(pieces, links, patterns):
        rows = pattern_rows(pattern, level)
        stack = stack_blocks(piece, len(rows))
        product = dot(stack, link[...]) if level == 1 else dot_turned(stack, link[...])
        part = masked_sum(product, rows)
        total = part if total is None else total + part
    store_columns(out, total)


def apply_factor(full, factor):
    if factor.shape[0] < full.shape[1]:
        return dot_turned(full, factor[...])
    return dot(full, factor[...])


def back_product(level, full, link, pattern):
    rows = pattern_rows(pattern, level)
    stacked = jnp.concatenate([full * row for row in rows], axis=0).astype(BF16)
    product = apply_factor(stacked, link)
    block = lanes((HALF, product.shape[1])) // BLOCK
    total = product[:HALF]
    for index in range(1, len(rows)):
        part = product[index * HALF : (index + 1) * HALF]
        total = jnp.where(block == index, part, total)
    return total


def store_copies(out, value):
    value = value.astype(BF16)
    for index in range(out.shape[0]):
        out[index] = value


def joined(gathered):
    return jnp.concatenate([gathered[index] for index in range(gathered.shape[0])], axis=1)


def in_kernel(
    received, own_pattern, other_pattern, own_lower, other_lower, own_link, other_link,
    own_out, other_out, rows_out, out, turned,
):
    flat = received[...].reshape(1024, 128)
    turned[...] = flat.astype(F32).T.astype(BF16)
    info = received[pl.ds(lax.axis_index(LEAVES) * 4, 4)].astype(F32)
    rows = rows_of((1024, 128))
    lane = lanes((1, 128))
    fronts = []
    for chip in range(4):
        tile = info[chip]
        tails = (tile[7:8, :], tile[15:16, :])
        tail_high = jnp.where(lane < 64, tails[0], tails[1])
        tail_low = jnp.broadcast_to(jnp.where(lane < 64, tails[1], tails[0]), (8, 128))
        tail_low = pltpu.roll(tail_low, 64, 1)[0:1, :]
        positions = (
            tile[5:6, :] * 8.0 + tile[6:7, :],
            tail_high * 8.0 + tail_low,
            tile[13:14, :] * 8.0 + tile[14:15, :],
        )
        hot = jnp.concatenate(
            [one_hot(rows == position.astype(jnp.int32)) for position in positions], axis=1
        )
        picked = dot(turned[chip * 32 : (chip + 1) * 32, :], hot)
        fronts.append(
            jnp.where(lanes((HALF, 384)) < LEAF, picked[:HALF], picked[HALF:]).astype(BF16)
        )
    start = pl.multiple_of(lax.axis_index("x") * 32, 32)
    rows_out[...] = turned[pl.ds(start, 32), :]
    front = jnp.concatenate(fronts, axis=1)
    own = apply_factor(front, own_lower).astype(BF16)
    other = apply_factor(front, other_lower).astype(BF16)
    own_out[...] = own
    other_out[...] = other
    pieces = (own.astype(F32), other.astype(F32))
    down_product(1, pieces, (own_link, other_link), (own_pattern, other_pattern), out)


def rest_kernel(turned, own_owner, other_owner, first_out, second_out, third_out):
    core = core_index()
    parts = []
    for owner, which in ((own_owner, core), (other_owner, 1 - core)):
        source, turn = source_and_turn(owner[1:2, :640])
        hot = one_hot(rows_of((1024, 640)) == source * 8 + turn)
        rows = turned[pl.ds(pl.multiple_of(which * HALF, HALF), HALF), :]
        parts.append(dot(rows, hot))
    offset = LEAF
    for out in (first_out, second_out, third_out):
        width = out.shape[1] // 2
        own, other = (part[:, offset : offset + width] for part in parts)
        out[...] = in_order(own, other).astype(BF16)
        offset += width


def reduce_kernel(level, received, right, masks, out):
    share = received[0].astype(F32)
    for index in range(1, received.shape[0]):
        share = share + received[index].astype(F32)
    store_copies(out, (right[...].astype(F32) - share) * chip_mask(masks, level))


def solve_pieces(level, gathered, masks, own_factor, other_factor):
    full = joined(gathered)
    own_mask, other_mask = piece_masks(masks, level)
    own = (apply_factor(full, own_factor) * own_mask).astype(BF16)
    other = (apply_factor(full, other_factor) * other_mask).astype(BF16)
    return own, other


def up_kernel(
    level, gathered, masks, own_pattern, other_pattern, own_lower, other_lower, own_link,
    other_link, own_out, other_out, out,
):
    own, other = solve_pieces(level, gathered, masks, own_lower, other_lower)
    own_out[...] = own
    other_out[...] = other
    pieces = (own.astype(F32), other.astype(F32))
    links = (own_link, other_link)
    down_product(level + 1, pieces, links, (own_pattern, other_pattern), out)


def solve_kernel(level, gathered, masks, own_factor, other_factor, own_out, other_out, out):
    own, other = solve_pieces(level, gathered, masks, own_factor, other_factor)
    own_out[...] = own
    other_out[...] = other
    store_copies(out, in_order(own.astype(F32), other.astype(F32)))


def top_kernel(level, gathered, masks, own_factor, other_factor, out):
    own, other = solve_pieces(level, gathered, masks, own_factor, other_factor)
    store_copies(out, in_order(own.astype(F32), other.astype(F32)))


def back_kernel(
    level, gathered, masks, own_pattern, other_pattern, own_y, other_y, own_link, other_link, out
):
    full = joined(gathered).astype(F32)
    own = own_y[...].astype(F32) - back_product(level + 1, full, own_link, own_pattern)
    other = other_y[...].astype(F32) - back_product(level + 1, full, other_link, other_pattern)
    if level:
        own_mask, other_mask = piece_masks(masks, level)
        own = own * own_mask
        other = other * other_mask
    store_copies(out, in_order(own, other))


def out_kernel(
    gathered, own_owner, other_owner, own_first, other_first, own_second, other_second,
    own_third, other_third, own_upper, other_upper, out,
):
    core = core_index()
    full = joined(gathered)
    tails = ((own_first, own_second, own_third), (other_first, other_second, other_third))
    placed = []
    uppers = (own_upper, other_upper)
    for which, owner in enumerate((own_owner, other_owner)):
        source, turn = source_and_turn(owner[1:2, :640])
        slot = (source & 1) * 512 + (source >> 1) * 8 + turn
        hot = one_hot(rows_of((1024, 640)) == slot)
        leaf = apply_factor(full, uppers[which])
        front = jnp.concatenate([leaf] + [tail[...].astype(F32) for tail in tails[which]], axis=1)
        total = dot_turned(front.astype(BF16), hot)
        placed.append(jnp.concatenate([total[:, :512], total[:, 512:]], axis=0))
    first = jnp.where(core == 0, placed[0], placed[1])
    second = jnp.where(core == 0, placed[1], placed[0])
    unused = jnp.zeros((64, 512), F32)
    stacked = jnp.concatenate([first, second, unused], axis=0)
    out[...] = stacked.T.reshape(64, 8, 128).astype(BF16)


def final_kernel(received, own_columns, other_columns, own_out, other_out):
    core = core_index()
    turned = received[...].reshape(512, 128).astype(F32).T
    first = jnp.concatenate([turned[:HALF], turned[2 * HALF : 3 * HALF]], axis=1)
    second = jnp.concatenate([turned[HALF : 2 * HALF], turned[3 * HALF : 4 * HALF]], axis=1)
    own = jnp.where(core == 0, first, second).astype(BF16)
    other = jnp.where(core == 0, second, first).astype(BF16)
    work = ((own, own_columns, own_out), (other, other_columns, other_out))
    for value, columns, out in work:
        hot = one_hot(rows_of((640, 1024)) == columns[0:1, :])
        out[...] = dot_turned(value, hot).astype(BF16)


def per_device(
    right_side,
    send_order,
    owner_order,
    live_rows,
    lower_leaf,
    upper_leaf,
    lower_first,
    lower_second,
    lower_third,
    upper_first,
    upper_second,
    upper_third,
    downlink_first,
    downlink_second,
    downlink_third,
    uplink_first,
    uplink_second,
    uplink_third,
    pattern_first,
    pattern_second,
    pattern_third,
):
    core = lax.axis_index("c")
    factors = {
        "lower1": lower_first,
        "down2": downlink_second,
        "lower2": lower_second,
        "down3": downlink_third,
        "lower3": lower_third.T,
        "upper3": upper_third.T,
        "back3": uplink_third,
        "upper2": upper_second,
        "back2": uplink_second,
        "upper1": upper_first,
        "back1": uplink_first.T,
        "upper0": upper_leaf.T,
    }
    pairs = {}

    def begin(value, names):
        tied = lax.optimization_barrier((value,) + tuple(factors[name] for name in names))
        for name, factor in zip(names, tied[1:]):
            pairs[name] = (factors[name], swap(factor))
        return tied[0]

    def finish(value, names):
        tied = lax.optimization_barrier((value,) + tuple(pairs[name][1] for name in names))
        for name, other in zip(names, tied[1:]):
            pairs[name] = (pairs[name][0], other)
        return tied[0]

    mine, theirs, own_patterns, masks, own_columns, own_lower, own_link = call(
        start_kernel,
        "start",
        [
            ((16, 8, 128), BF16),
            ((16, 8, 128), BF16),
            ((16, SEP), BF16),
            ((8, 896), F32),
            ((8, 1024), jnp.int32),
            ((LEAF, 8 * LEAF), BF16),
            ((LEAF, SEP), BF16),
        ],
        (),
        distant=(
            live_rows,
            send_order,
            owner_order,
            right_side,
            pattern_first.T,
            pattern_second.T,
            pattern_third.T,
            lower_leaf.T,
            downlink_first.T,
        ),
        scratch=[
            pltpu.SMEM((14,), jnp.int32),
            pltpu.VMEM((640,), jnp.int32),
            pltpu.VMEM((640,), jnp.int32),
            pltpu.VMEM((32, 640), BF16),
            pltpu.VMEM((3, BLOCK), jnp.int32),
            pltpu.VMEM((4, BLOCK), jnp.int32),
            pltpu.VMEM((2, BLOCK), jnp.int32),
        ],
    )
    factors["lower0"] = own_lower
    factors["down1"] = own_link
    other_columns = swap(own_columns)
    other_patterns = swap(own_patterns)
    payload = call(
        pack_kernel, "pack_rows", [((16, 4, 16, 128), BF16)], (mine, swap(theirs))
    )[0]
    payload, other_columns, other_patterns = lax.optimization_barrier(
        (payload, other_columns, other_patterns)
    )
    patterns = (own_patterns, other_patterns)
    payload = begin(payload, FIRST)
    received = finish(exchange(payload.reshape(64, 16, 128), 4), FIRST)
    own_y, other_y, own_rows, term = call(
        in_kernel,
        "leaf_front",
        [
            ((HALF, LEAF), BF16),
            ((HALF, LEAF), BF16),
            ((32, 1024), BF16),
            ((8, HALF, 512), BF16),
        ],
        (received,) + patterns + pairs["lower0"] + pairs["down1"],
        scratch=[pltpu.VMEM((128, 1024), BF16)],
    )
    level_y = {0: (own_y, other_y)}
    rights = call(
        rest_kernel,
        "separator_rows",
        [((HALF, 512), BF16), ((HALF, 256), BF16), ((HALF, 128), BF16)],
        (own_rows, own_columns, other_columns),
    )
    for level in (1, 2, 3):
        members = MEMBERS[level]
        chip_width = SEP // members
        piece = ((HALF, WIDTHS[level]), BF16)
        if level == 1:
            term, rights = lax.optimization_barrier((term, rights))
            term = begin(term, SECOND)
        shared = exchange(term, level)
        reduced = call(
            functools.partial(reduce_kernel, level),
            "reduce_%d" % level,
            [((members, HALF, chip_width), BF16)],
            (shared, rights[level - 1], masks),
        )[0]
        if level == 1:
            reduced = begin(finish(reduced, SECOND), THIRD)
        elif level == 2:
            reduced = begin(finish(reduced, THIRD), FOURTH)
        else:
            reduced = finish(reduced, FOURTH)
        gathered = exchange(reduced, level)
        if level < 3:
            above = MEMBERS[level + 1]
            own_y, other_y, term = call(
                functools.partial(up_kernel, level),
                "up_%d" % level,
                [piece, piece, ((above, HALF, SEP // above), BF16)],
                (gathered, masks)
                + patterns
                + pairs["lower%d" % level]
                + pairs["down%d" % (level + 1)],
            )
        else:
            copies = call(
                functools.partial(top_kernel, level),
                "top_lower",
                [((members, HALF, chip_width), BF16)],
                (gathered, masks) + pairs["lower3"],
            )[0]
            break
        level_y[level] = (own_y, other_y)
    level_x = {}
    for level in (3, 2, 1):
        members = MEMBERS[level]
        chip_width = SEP // members
        piece = ((HALF, WIDTHS[level]), BF16)
        gathered = exchange(copies, level)
        own_x, other_x, copies = call(
            functools.partial(solve_kernel, level),
            "solve_%d" % level,
            [piece, piece, ((members, HALF, chip_width), BF16)],
            (gathered, masks) + pairs["upper%d" % level],
        )
        level_x[level] = (own_x, other_x)
        gathered = exchange(copies, level)
        below = level - 1
        copies = call(
            functools.partial(back_kernel, below),
            "back_%d" % below,
            [((MEMBERS[below], HALF, 2 * WIDTHS[below]), BF16)],
            (gathered, masks) + patterns + level_y[below] + pairs["back%d" % level],
        )[0]
    gathered = exchange(copies, 0)
    outbound = call(
        out_kernel,
        "leaf_solution",
        [((64, 8, 128), BF16)],
        (gathered, own_columns, other_columns)
        + level_x[1]
        + level_x[2]
        + level_x[3]
        + pairs["upper0"],
    )[0]
    returned = exchange(outbound, 4)
    own_half, other_half = call(
        final_kernel,
        "natural_order",
        [((HALF, 640), BF16), ((HALF, 640), BF16)],
        (returned, own_columns, other_columns),
    )
    far_half = swap(other_half)
    return jnp.where(
        core == 0,
        jnp.concatenate([own_half, far_half]),
        jnp.concatenate([far_half, own_half]),
    )


def solution(mesh):
    fine = Mesh(mesh.devices.reshape(2, 2, 2, 2, 4, 2), EVERY)
    by_column = P(None, EVERY)
    placed = (by_column, P(EVERY), P(EVERY), P()) + (by_column,) * 17
    return jax.shard_map(
        per_device, mesh=fine, in_specs=placed, out_specs=by_column, check_vma=False
    )
```

```python
import functools

import jax
import jax.numpy as jnp
from jax import lax
from jax.experimental import pallas as pl
from jax.experimental.pallas import tpu as pltpu
from jax.sharding import Mesh, PartitionSpec as P

EVERY = ("z1", "z0", "y1", "y0", "x", "c")
LEAVES = ("z1", "z0", "y1", "y0")
CHIPS = {
    0: ("x",),
    1: ("y0", "x"),
    2: ("y1", "y0", "x"),
    3: ("z0", "y1", "y0", "x"),
    4: ("z1", "z0", "y1", "y0", "x"),
}
MEMBERS = {0: 4, 1: 8, 2: 16, 3: 32, 4: 64}
FIRST = ("lower0", "down1", "lower1", "down2")
SECOND = ("lower2", "down3")
THIRD = ("lower3", "upper3", "back3", "upper2")
FOURTH = ("back2", "upper1", "back1", "upper0")
HALF = 16
SEP = 4096
BLOCK = 64
LEAF = 192
WIDTHS = {0: 192, 1: 256, 2: 128, 3: 64}
FIRST_NODE = {1: 0, 2: 8, 3: 12}
F32 = jnp.float32
BF16 = jnp.bfloat16
VMEM_SPEC = pl.BlockSpec(memory_space=pltpu.VMEM)
HBM_SPEC = pl.BlockSpec(memory_space=pltpu.HBM)


def swap(value):
    return lax.ppermute(value, "c", [(0, 1), (1, 0)])


def exchange(value, level):
    return lax.all_to_all(value, CHIPS[level], split_axis=0, concat_axis=0, tiled=True)


def call(body, name, outs, operands, distant=(), scratch=()):
    constrained = [pltpu.with_memory_space_constraint(value, pltpu.HBM) for value in distant]
    scratch = list(scratch)
    if distant:
        scratch.append(pltpu.SemaphoreType.DMA((len(distant),)))
    return pl.pallas_call(
        body,
        name=name,
        out_shape=[jax.ShapeDtypeStruct(shape, dtype) for shape, dtype in outs],
        in_specs=[HBM_SPEC] * len(distant) + [VMEM_SPEC] * len(operands),
        out_specs=[VMEM_SPEC] * len(outs),
        scratch_shapes=scratch,
        compiler_params=pltpu.CompilerParams(vmem_limit_bytes=12 * 1024 * 1024),
    )(*constrained, *operands)


def fetch(sources, buffers, semaphores):
    copies = [
        pltpu.make_async_copy(source, buffer, semaphores.at[index])
        for index, (source, buffer) in enumerate(zip(sources, buffers))
    ]
    for copy in copies:
        copy.start()
    return copies


def dot(left, right):
    return jnp.dot(left, right, preferred_element_type=F32)


def lanes(shape):
    return lax.broadcasted_iota(jnp.int32, shape, len(shape) - 1)


def rows_of(shape):
    return lax.broadcasted_iota(jnp.int32, shape, 0)


def one_hot(matches):
    return jnp.where(matches, 1.0, 0.0).astype(BF16)


def dot_turned(left, right):
    return lax.dot_general(left, right, (((1,), (1,)), ((), ())), preferred_element_type=F32)


def core_index():
    return lax.axis_index("c")


def source_and_turn(order):
    source = (order * 6554) >> 15
    return source, order - source * 5


def in_order(own, other):
    core = core_index()
    first = jnp.where(core == 0, own, other)
    second = jnp.where(core == 0, other, own)
    return jnp.concatenate([first, second], axis=1)


def chip_mask(masks, level):
    start = {1: 0, 2: 512, 3: 768}[level]
    return masks[0:1, start : start + 2 * WIDTHS[level]]


def piece_masks(masks, level):
    width = WIDTHS[level]
    whole = chip_mask(masks, level)
    core = core_index()
    first = whole[:, :width]
    second = whole[:, width:]
    return jnp.where(core == 0, first, second), jnp.where(core == 0, second, first)


def pattern_rows(patterns, level):
    start = {1: 0, 2: 3, 3: 7}[level]
    count = {1: 3, 2: 4, 3: 2}[level]
    return [patterns[start + row : start + row + 1, :].astype(F32) for row in range(count)]


def pick_rows(send_order, owner_order, right, mine, theirs):
    core = core_index()
    send = send_order[...].reshape(1, 640)
    owner = owner_order[...].reshape(1, 640)
    natural = dot(right[...], one_hot(rows_of((640, 640)) == send)).astype(BF16)
    lane = lanes((1, 1024))
    turn = lane & 7
    wanted = (((lane >> 3) & 15) * 8 + (lane >> 7)) * 5 + turn
    wanted = jnp.where(turn < 5, wanted, -1)
    picked = dot(natural, one_hot(rows_of((640, 1024)) == wanted))
    source, turn = source_and_turn(owner)
    high = jnp.broadcast_to(source[:, :256].astype(F32), (8, 256))
    low = jnp.broadcast_to(turn[:, :256].astype(F32), (8, 256))
    high_left = pltpu.roll(high, 192, 1)[:, :128]
    low_left = pltpu.roll(low, 192, 1)[:, :128]
    high_right = pltpu.roll(high, 64, 1)[:, :128]
    main_high = jnp.where(core == 0, high[:, :128], high_left)
    main_low = jnp.where(core == 0, low[:, :128], low_left)
    lane = lanes((8, 128))
    tail = jnp.where(
        core == 0,
        jnp.where(lane < 64, high[:, 128:], low_left),
        jnp.where(lane < 64, low[:, :128], high_right),
    )
    row = rows_of((8, 128))
    info = jnp.where(row == 5, main_high, 0.0)
    info = jnp.where(row == 6, main_low, info)
    info = jnp.where(row == 7, tail, info)
    tiles = []
    for half in range(2):
        part = picked[half * HALF : (half + 1) * HALF]
        stacked = jnp.concatenate([part[:, f * 128 : (f + 1) * 128] for f in range(8)], axis=0)
        tiles.append(stacked.T.reshape(16, 8, 128) + info[None])
    mine[...] = jnp.where(core == 0, tiles[0], tiles[1]).astype(BF16)
    theirs[...] = jnp.where(core == 0, tiles[1], tiles[0]).astype(BF16)


def pack_kernel(mine, other, out):
    core = core_index()
    own = mine[...].astype(F32)
    far = other[...].astype(F32)
    first = jnp.where(core == 0, own, far)
    second = jnp.where(core == 0, far, own)
    tiles = jnp.concatenate([first, second], axis=1).astype(BF16)
    for copy in range(4):
        out[:, copy] = tiles


def make_tables(live, send_order, owner_order, first, second, third, wide, masks, columns):
    hot = one_hot(lanes((BLOCK, SEP)) // BLOCK == rows_of((BLOCK, SEP)))
    start = 0
    wide[...] = jnp.zeros_like(wide)
    for pattern in (first, second, third):
        count = pattern.shape[0]
        wide[start : start + count, :] = dot(
            pattern[...].astype(F32).astype(BF16), hot
        ).astype(BF16)
        start += count
    leaf = lax.axis_index(LEAVES)
    chip = lax.axis_index("x")
    for level, start in ((1, 0), (2, 512), (3, 768)):
        width = 2 * WIDTHS[level]
        member = leaf & (2**level - 1)
        row = (member * 4 + chip) * width + lanes((8, width))
        count = live[FIRST_NODE[level] + (leaf >> level)]
        masks[:, start : start + width] = (row < count).astype(F32)
    lane = lanes((1, 1024))
    turn = lane & 7
    device = ((lane >> 3) & 63) * 2 + (lane >> 9)
    wanted = jnp.where(turn < 5, device * 5 + turn, -1)
    hot = one_hot(rows_of((640, 1024)) == wanted)
    send = send_order[...].reshape(1, 640) + 1
    stacked = jnp.concatenate(
        [
            jnp.broadcast_to(digit.astype(F32), (8, 640))
            for digit in (send >> 3, send & 7)
        ],
        axis=0,
    )
    placed = dot(stacked.astype(BF16), hot)
    row = rows_of((8, 1024))
    owner = jnp.broadcast_to(owner_order[...].reshape(1, 640), (8, 640))
    owner = jnp.concatenate([owner, jnp.zeros((8, 384), jnp.int32)], axis=1)
    values = (placed[:8] * 8.0 + placed[8:]).astype(jnp.int32) - 1
    columns[...] = jnp.where(row == 0, values, owner)


def start_kernel(
    live, send_order, owner_order, right, first, second, third, lower, link, mine, theirs, wide,
    masks, columns, lower_out, link_out, live_buffer, send_buffer, owner_buffer, right_buffer,
    first_buffer, second_buffer, third_buffer, semaphores,
):
    buffers = (
        live_buffer, send_buffer, owner_buffer, right_buffer, first_buffer, second_buffer,
        third_buffer, lower_out, link_out,
    )
    sources = (live, send_order, owner_order, right, first, second, third, lower, link)
    copies = fetch(sources, buffers, semaphores)
    for copy in copies[:7]:
        copy.wait()
    pick_rows(send_buffer, owner_buffer, right_buffer, mine, theirs)
    make_tables(
        live_buffer, send_buffer, owner_buffer, first_buffer, second_buffer, third_buffer, wide,
        masks, columns,
    )
    for copy in copies[7:]:
        copy.wait()


def stack_blocks(piece, count):
    block = lanes(piece.shape) // BLOCK
    zero = jnp.zeros_like(piece)
    return jnp.concatenate(
        [jnp.where(block == index, piece, zero) for index in range(count)], axis=0
    ).astype(BF16)


def masked_sum(product, rows):
    total = None
    for index, row in enumerate(rows):
        part = product[index * HALF : (index + 1) * HALF] * row
        total = part if total is None else total + part
    return total


def store_columns(out, value):
    width = out.shape[2]
    value = value.astype(BF16)
    for index in range(out.shape[0]):
        out[index] = value[:, index * width : (index + 1) * width]


def down_product(level, pieces, links, patterns, out):
    total = None
    for piece, link, pattern in zip(pieces, links, patterns):
        rows = pattern_rows(pattern, level)
        stack = stack_blocks(piece, len(rows))
        product = dot(stack, link[...]) if level == 1 else dot_turned(stack, link[...])
        part = masked_sum(product, rows)
        total = part if total is None else total + part
    store_columns(out, total)


def apply_factor(full, factor):
    if factor.shape[0] < full.shape[1]:
        return dot_turned(full, factor[...])
    return dot(full, factor[...])


def back_product(level, full, link, pattern):
    rows = pattern_rows(pattern, level)
    stacked = jnp.concatenate([full * row for row in rows], axis=0).astype(BF16)
    product = apply_factor(stacked, link)
    block = lanes((HALF, product.shape[1])) // BLOCK
    total = product[:HALF]
    for index in range(1, len(rows)):
        part = product[index * HALF : (index + 1) * HALF]
        total = jnp.where(block == index, part, total)
    return total


def store_copies(out, value):
    value = value.astype(BF16)
    for index in range(out.shape[0]):
        out[index] = value


def joined(gathered):
    return jnp.concatenate([gathered[index] for index in range(gathered.shape[0])], axis=1)


def in_kernel(
    received, own_pattern, other_pattern, own_lower, other_lower, own_link, other_link,
    own_out, other_out, rows_out, out, turned,
):
    flat = received[...].reshape(1024, 128)
    turned[...] = flat.astype(F32).T.astype(BF16)
    info = received[pl.ds(lax.axis_index(LEAVES) * 4, 4)].astype(F32)
    rows = rows_of((1024, 128))
    lane = lanes((1, 128))
    fronts = []
    for chip in range(4):
        tile = info[chip]
        tails = (tile[7:8, :], tile[15:16, :])
        tail_high = jnp.where(lane < 64, tails[0], tails[1])
        tail_low = jnp.broadcast_to(jnp.where(lane < 64, tails[1], tails[0]), (8, 128))
        tail_low = pltpu.roll(tail_low, 64, 1)[0:1, :]
        positions = (
            tile[5:6, :] * 8.0 + tile[6:7, :],
            tail_high * 8.0 + tail_low,
            tile[13:14, :] * 8.0 + tile[14:15, :],
        )
        hot = jnp.concatenate(
            [one_hot(rows == position.astype(jnp.int32)) for position in positions], axis=1
        )
        picked = dot(turned[chip * 32 : (chip + 1) * 32, :], hot)
        fronts.append(
            jnp.where(lanes((HALF, 384)) < LEAF, picked[:HALF], picked[HALF:]).astype(BF16)
        )
    start = pl.multiple_of(lax.axis_index("x") * 32, 32)
    rows_out[...] = turned[pl.ds(start, 32), :]
    front = jnp.concatenate(fronts, axis=1)
    own = apply_factor(front, own_lower).astype(BF16)
    other = apply_factor(front, other_lower).astype(BF16)
    own_out[...] = own
    other_out[...] = other
    pieces = (own.astype(F32), other.astype(F32))
    down_product(1, pieces, (own_link, other_link), (own_pattern, other_pattern), out)


def rest_kernel(turned, own_owner, other_owner, first_out, second_out, third_out):
    core = core_index()
    parts = []
    for owner, which in ((own_owner, core), (other_owner, 1 - core)):
        source, turn = source_and_turn(owner[1:2, :640])
        hot = one_hot(rows_of((1024, 640)) == source * 8 + turn)
        rows = turned[pl.ds(pl.multiple_of(which * HALF, HALF), HALF), :]
        parts.append(dot(rows, hot))
    offset = LEAF
    for out in (first_out, second_out, third_out):
        width = out.shape[1] // 2
        own, other = (part[:, offset : offset + width] for part in parts)
        out[...] = in_order(own, other).astype(BF16)
        offset += width


def reduce_kernel(level, received, right, masks, out):
    share = received[0].astype(F32)
    for index in range(1, received.shape[0]):
        share = share + received[index].astype(F32)
    store_copies(out, (right[...].astype(F32) - share) * chip_mask(masks, level))


def solve_pieces(level, gathered, masks, own_factor, other_factor):
    full = joined(gathered)
    own_mask, other_mask = piece_masks(masks, level)
    own = (apply_factor(full, own_factor) * own_mask).astype(BF16)
    other = (apply_factor(full, other_factor) * other_mask).astype(BF16)
    return own, other


def up_kernel(
    level, gathered, masks, own_pattern, other_pattern, own_lower, other_lower, own_link,
    other_link, own_out, other_out, out,
):
    own, other = solve_pieces(level, gathered, masks, own_lower, other_lower)
    own_out[...] = own
    other_out[...] = other
    pieces = (own.astype(F32), other.astype(F32))
    links = (own_link, other_link)
    down_product(level + 1, pieces, links, (own_pattern, other_pattern), out)


def solve_kernel(level, gathered, masks, own_factor, other_factor, own_out, other_out, out):
    own, other = solve_pieces(level, gathered, masks, own_factor, other_factor)
    own_out[...] = own
    other_out[...] = other
    store_copies(out, in_order(own.astype(F32), other.astype(F32)))


def top_kernel(level, gathered, masks, own_factor, other_factor, out):
    own, other = solve_pieces(level, gathered, masks, own_factor, other_factor)
    store_copies(out, in_order(own.astype(F32), other.astype(F32)))


def back_kernel(
    level, gathered, masks, own_pattern, other_pattern, own_y, other_y, own_link, other_link, out
):
    full = joined(gathered).astype(F32)
    own = own_y[...].astype(F32) - back_product(level + 1, full, own_link, own_pattern)
    other = other_y[...].astype(F32) - back_product(level + 1, full, other_link, other_pattern)
    if level:
        own_mask, other_mask = piece_masks(masks, level)
        own = own * own_mask
        other = other * other_mask
        store_copies(out, in_order(own, other))
    else:
        out[...] = in_order(own, other).astype(BF16)


def out_kernel(
    own_part, first_part, second_part, third_part, own_owner, other_owner, own_first, other_first,
    own_second, other_second, own_third, other_third, own_upper, other_upper, out, row,
):
    chip = lax.axis_index("x")
    core = core_index()
    for step, part in enumerate((own_part, first_part, second_part, third_part)):
        start = pl.multiple_of((chip ^ step) * (2 * LEAF), 128)
        row[:, pl.ds(start, 2 * LEAF)] = part[...]
    full = row[...]
    tails = ((own_first, own_second, own_third), (other_first, other_second, other_third))
    placed = []
    uppers = (own_upper, other_upper)
    for which, owner in enumerate((own_owner, other_owner)):
        source, turn = source_and_turn(owner[1:2, :640])
        slot = (source & 1) * 512 + (source >> 1) * 8 + turn
        hot = one_hot(rows_of((1024, 640)) == slot)
        leaf = apply_factor(full, uppers[which])
        front = jnp.concatenate([leaf] + [tail[...].astype(F32) for tail in tails[which]], axis=1)
        total = dot_turned(front.astype(BF16), hot)
        placed.append(jnp.concatenate([total[:, :512], total[:, 512:]], axis=0))
    first = jnp.where(core == 0, placed[0], placed[1])
    second = jnp.where(core == 0, placed[1], placed[0])
    unused = jnp.zeros((64, 512), F32)
    stacked = jnp.concatenate([first, second, unused], axis=0)
    out[...] = stacked.T.reshape(64, 8, 128).astype(BF16)


def final_kernel(received, far, columns, out):
    core = core_index()
    halves = []
    for ref in (received, far):
        turned = ref[...].reshape(512, 128).astype(F32).T
        first = jnp.concatenate([turned[:HALF], turned[2 * HALF : 3 * HALF]], axis=1)
        second = jnp.concatenate([turned[HALF : 2 * HALF], turned[3 * HALF : 4 * HALF]], axis=1)
        halves.append(jnp.where(core == 0, first, second))
    top = jnp.where(core == 0, halves[0], halves[1])
    bottom = jnp.where(core == 0, halves[1], halves[0])
    value = jnp.concatenate([top, bottom], axis=0).astype(BF16)
    hot = one_hot(rows_of((640, 1024)) == columns[0:1, :])
    out[...] = dot_turned(value, hot).astype(BF16)


def per_device(
    right_side,
    send_order,
    owner_order,
    live_rows,
    lower_leaf,
    upper_leaf,
    lower_first,
    lower_second,
    lower_third,
    upper_first,
    upper_second,
    upper_third,
    downlink_first,
    downlink_second,
    downlink_third,
    uplink_first,
    uplink_second,
    uplink_third,
    pattern_first,
    pattern_second,
    pattern_third,
):
    factors = {
        "lower1": lower_first,
        "down2": downlink_second,
        "lower2": lower_second,
        "down3": downlink_third,
        "lower3": lower_third.T,
        "upper3": upper_third.T,
        "back3": uplink_third,
        "upper2": upper_second,
        "back2": uplink_second,
        "upper1": upper_first,
        "back1": uplink_first.T,
        "upper0": upper_leaf.T,
    }
    pairs = {}

    def begin(value, names):
        tied = lax.optimization_barrier((value,) + tuple(factors[name] for name in names))
        for name, factor in zip(names, tied[1:]):
            pairs[name] = (factors[name], swap(factor))
        return tied[0]

    def finish(value, names):
        tied = lax.optimization_barrier((value,) + tuple(pairs[name][1] for name in names))
        for name, other in zip(names, tied[1:]):
            pairs[name] = (pairs[name][0], other)
        return tied[0]

    mine, theirs, own_patterns, masks, own_columns, own_lower, own_link = call(
        start_kernel,
        "start",
        [
            ((16, 8, 128), BF16),
            ((16, 8, 128), BF16),
            ((16, SEP), BF16),
            ((8, 896), F32),
            ((8, 1024), jnp.int32),
            ((LEAF, 8 * LEAF), BF16),
            ((LEAF, SEP), BF16),
        ],
        (),
        distant=(
            live_rows,
            send_order,
            owner_order,
            right_side,
            pattern_first.T,
            pattern_second.T,
            pattern_third.T,
            lower_leaf.T,
            downlink_first.T,
        ),
        scratch=[
            pltpu.SMEM((14,), jnp.int32),
            pltpu.VMEM((640,), jnp.int32),
            pltpu.VMEM((640,), jnp.int32),
            pltpu.VMEM((32, 640), BF16),
            pltpu.VMEM((3, BLOCK), jnp.int32),
            pltpu.VMEM((4, BLOCK), jnp.int32),
            pltpu.VMEM((2, BLOCK), jnp.int32),
        ],
    )
    factors["lower0"] = own_lower
    factors["down1"] = own_link
    other_columns = swap(own_columns)
    other_patterns = swap(own_patterns)
    payload = call(
        pack_kernel, "pack_rows", [((16, 4, 16, 128), BF16)], (mine, swap(theirs))
    )[0]
    payload, other_columns, other_patterns = lax.optimization_barrier(
        (payload, other_columns, other_patterns)
    )
    patterns = (own_patterns, other_patterns)
    payload = begin(payload, FIRST)
    received = finish(exchange(payload.reshape(64, 16, 128), 4), FIRST)
    own_y, other_y, own_rows, term = call(
        in_kernel,
        "leaf_front",
        [
            ((HALF, LEAF), BF16),
            ((HALF, LEAF), BF16),
            ((32, 1024), BF16),
            ((8, HALF, 512), BF16),
        ],
        (received,) + patterns + pairs["lower0"] + pairs["down1"],
        scratch=[pltpu.VMEM((128, 1024), BF16)],
    )
    level_y = {0: (own_y, other_y)}
    rights = call(
        rest_kernel,
        "separator_rows",
        [((HALF, 512), BF16), ((HALF, 256), BF16), ((HALF, 128), BF16)],
        (own_rows, own_columns, other_columns),
    )
    for level in (1, 2, 3):
        members = MEMBERS[level]
        chip_width = SEP // members
        piece = ((HALF, WIDTHS[level]), BF16)
        if level == 1:
            term, rights = lax.optimization_barrier((term, rights))
            term = begin(term, SECOND)
        shared = exchange(term, level)
        reduced = call(
            functools.partial(reduce_kernel, level),
            "reduce_%d" % level,
            [((members, HALF, chip_width), BF16)],
            (shared, rights[level - 1], masks),
        )[0]
        if level == 1:
            reduced = begin(finish(reduced, SECOND), THIRD)
        elif level == 2:
            reduced = begin(finish(reduced, THIRD), FOURTH)
        else:
            reduced = finish(reduced, FOURTH)
        gathered = exchange(reduced, level)
        if level < 3:
            above = MEMBERS[level + 1]
            own_y, other_y, term = call(
                functools.partial(up_kernel, level),
                "up_%d" % level,
                [piece, piece, ((above, HALF, SEP // above), BF16)],
                (gathered, masks)
                + patterns
                + pairs["lower%d" % level]
                + pairs["down%d" % (level + 1)],
            )
        else:
            copies = call(
                functools.partial(top_kernel, level),
                "top_lower",
                [((members, HALF, chip_width), BF16)],
                (gathered, masks) + pairs["lower3"],
            )[0]
            break
        level_y[level] = (own_y, other_y)
    level_x = {}
    for level in (3, 2, 1):
        members = MEMBERS[level]
        chip_width = SEP // members
        piece = ((HALF, WIDTHS[level]), BF16)
        gathered = exchange(copies, level)
        own_x, other_x, copies = call(
            functools.partial(solve_kernel, level),
            "solve_%d" % level,
            [piece, piece, ((members, HALF, chip_width), BF16)],
            (gathered, masks) + pairs["upper%d" % level],
        )
        level_x[level] = (own_x, other_x)
        gathered = exchange(copies, level)
        below = level - 1
        shape = (HALF, 2 * WIDTHS[below])
        copies = call(
            functools.partial(back_kernel, below),
            "back_%d" % below,
            [((MEMBERS[below],) + shape if below else shape, BF16)],
            (gathered, masks) + patterns + level_y[below] + pairs["back%d" % level],
        )[0]
    parts = [copies]
    for step in (1, 2, 3):
        ring = [(source, source ^ step) for source in range(4)]
        parts.append(lax.ppermute(copies, "x", ring))
    outbound = call(
        out_kernel,
        "leaf_solution",
        [((64, 8, 128), BF16)],
        tuple(parts)
        + (own_columns, other_columns)
        + level_x[1]
        + level_x[2]
        + level_x[3]
        + pairs["upper0"],
        scratch=[pltpu.VMEM((HALF, 8 * LEAF), BF16)],
    )[0]
    returned = exchange(outbound, 4)
    return call(
        final_kernel,
        "natural_order",
        [((2 * HALF, 640), BF16)],
        (returned, swap(returned), own_columns),
    )[0]


def solution(mesh):
    fine = Mesh(mesh.devices.reshape(2, 2, 2, 2, 4, 2), EVERY)
    by_column = P(None, EVERY)
    placed = (by_column, P(EVERY), P(EVERY), P()) + (by_column,) * 17
    return jax.shard_map(
        per_device, mesh=fine, in_specs=placed, out_specs=by_column, check_vma=False
    )
```

```python
import functools

import jax
import jax.numpy as jnp
from jax import lax
from jax.experimental import pallas as pl
from jax.experimental.pallas import tpu as pltpu
from jax.sharding import Mesh, PartitionSpec as P

EVERY = ("z1", "z0", "y1", "y0", "x", "c")
LEAVES = ("z1", "z0", "y1", "y0")
CHIPS = {
    0: ("x",),
    1: ("y0", "x"),
    2: ("y1", "y0", "x"),
    3: ("z0", "y1", "y0", "x"),
    4: ("z1", "z0", "y1", "y0", "x"),
}
MEMBERS = {0: 4, 1: 8, 2: 16, 3: 32, 4: 64}
FIRST = ("lower0", "down1", "lower1", "down2")
SECOND = ("lower2", "down3")
THIRD = ("lower3", "upper3", "back3", "upper2")
FOURTH = ("back2", "upper1", "back1", "upper0")
HALF = 16
SEP = 4096
BLOCK = 64
LEAF = 192
WIDTHS = {0: 192, 1: 256, 2: 128, 3: 64}
FIRST_NODE = {1: 0, 2: 8, 3: 12}
F32 = jnp.float32
BF16 = jnp.bfloat16
VMEM_SPEC = pl.BlockSpec(memory_space=pltpu.VMEM)
HBM_SPEC = pl.BlockSpec(memory_space=pltpu.HBM)


def swap(value):
    return lax.ppermute(value, "c", [(0, 1), (1, 0)])


def exchange(value, level):
    return lax.all_to_all(value, CHIPS[level], split_axis=0, concat_axis=0, tiled=True)


def call(body, name, outs, operands, distant=(), scratch=()):
    constrained = [pltpu.with_memory_space_constraint(value, pltpu.HBM) for value in distant]
    scratch = list(scratch)
    if distant:
        scratch.append(pltpu.SemaphoreType.DMA((len(distant),)))
    return pl.pallas_call(
        body,
        name=name,
        out_shape=[jax.ShapeDtypeStruct(shape, dtype) for shape, dtype in outs],
        in_specs=[HBM_SPEC] * len(distant) + [VMEM_SPEC] * len(operands),
        out_specs=[VMEM_SPEC] * len(outs),
        scratch_shapes=scratch,
        compiler_params=pltpu.CompilerParams(vmem_limit_bytes=12 * 1024 * 1024),
    )(*constrained, *operands)


def fetch(sources, buffers, semaphores):
    copies = [
        pltpu.make_async_copy(source, buffer, semaphores.at[index])
        for index, (source, buffer) in enumerate(zip(sources, buffers))
    ]
    for copy in copies:
        copy.start()
    return copies


def dot(left, right):
    return jnp.dot(left, right, preferred_element_type=F32)


def lanes(shape):
    return lax.broadcasted_iota(jnp.int32, shape, len(shape) - 1)


def rows_of(shape):
    return lax.broadcasted_iota(jnp.int32, shape, 0)


def one_hot(matches):
    return jnp.where(matches, 1.0, 0.0).astype(BF16)


def dot_turned(left, right):
    return lax.dot_general(left, right, (((1,), (1,)), ((), ())), preferred_element_type=F32)


def core_index():
    return lax.axis_index("c")


def source_and_turn(order):
    source = (order * 6554) >> 15
    return source, order - source * 5


def in_order(own, other):
    core = core_index()
    first = jnp.where(core == 0, own, other)
    second = jnp.where(core == 0, other, own)
    return jnp.concatenate([first, second], axis=1)


def chip_mask(masks, level):
    start = {1: 0, 2: 512, 3: 768}[level]
    return masks[0:1, start : start + 2 * WIDTHS[level]]


def piece_masks(masks, level):
    width = WIDTHS[level]
    whole = chip_mask(masks, level)
    core = core_index()
    first = whole[:, :width]
    second = whole[:, width:]
    return jnp.where(core == 0, first, second), jnp.where(core == 0, second, first)


def pattern_rows(patterns, level):
    start = {1: 0, 2: 3, 3: 7}[level]
    count = {1: 3, 2: 4, 3: 2}[level]
    return [patterns[start + row : start + row + 1, :].astype(F32) for row in range(count)]


def pick_rows(send_order, owner_order, right, order, mine, theirs):
    core = core_index()
    send = send_order[...].reshape(1, 640)
    owner = owner_order[...].reshape(1, 640)
    natural = dot(right[...], one_hot(rows_of((640, 640)) == send)).astype(BF16)
    picked = dot(natural, order)
    source, turn = source_and_turn(owner)
    high = jnp.broadcast_to(source[:, :256].astype(F32), (8, 256))
    low = jnp.broadcast_to(turn[:, :256].astype(F32), (8, 256))
    high_left = pltpu.roll(high, 192, 1)[:, :128]
    low_left = pltpu.roll(low, 192, 1)[:, :128]
    high_right = pltpu.roll(high, 64, 1)[:, :128]
    main_high = jnp.where(core == 0, high[:, :128], high_left)
    main_low = jnp.where(core == 0, low[:, :128], low_left)
    lane = lanes((8, 128))
    tail = jnp.where(
        core == 0,
        jnp.where(lane < 64, high[:, 128:], low_left),
        jnp.where(lane < 64, low[:, :128], high_right),
    )
    row = rows_of((8, 128))
    info = jnp.where(row == 5, main_high, 0.0)
    info = jnp.where(row == 6, main_low, info)
    info = jnp.where(row == 7, tail, info)
    tiles = []
    for half in range(2):
        part = picked[half * HALF : (half + 1) * HALF]
        stacked = jnp.concatenate([part[:, f * 128 : (f + 1) * 128] for f in range(8)], axis=0)
        tiles.append(stacked.T.reshape(16, 8, 128) + info[None])
    mine[...] = jnp.where(core == 0, tiles[0], tiles[1]).astype(BF16)
    theirs[...] = jnp.where(core == 0, tiles[1], tiles[0]).astype(BF16)


def pack_kernel(mine, other, out):
    core = core_index()
    own = mine[...].astype(F32)
    far = other[...].astype(F32)
    first = jnp.where(core == 0, own, far)
    second = jnp.where(core == 0, far, own)
    tiles = jnp.concatenate([first, second], axis=1).astype(BF16)
    for copy in range(4):
        out[:, copy] = tiles


def make_tables(
    live, send_order, owner_order, first, second, third, order, wide, masks, columns
):
    hot = one_hot(lanes((BLOCK, SEP)) // BLOCK == rows_of((BLOCK, SEP)))
    start = 0
    wide[...] = jnp.zeros_like(wide)
    for pattern in (first, second, third):
        count = pattern.shape[0]
        wide[start : start + count, :] = dot(
            pattern[...].astype(F32).astype(BF16), hot
        ).astype(BF16)
        start += count
    leaf = lax.axis_index(LEAVES)
    chip = lax.axis_index("x")
    for level, start in ((1, 0), (2, 512), (3, 768)):
        width = 2 * WIDTHS[level]
        member = leaf & (2**level - 1)
        row = (member * 4 + chip) * width + lanes((8, width))
        count = live[FIRST_NODE[level] + (leaf >> level)]
        masks[:, start : start + width] = (row < count).astype(F32)
    send = send_order[...].reshape(1, 640) + 1
    stacked = jnp.concatenate(
        [
            jnp.broadcast_to(digit.astype(F32), (8, 640))
            for digit in (send >> 3, send & 7)
        ],
        axis=0,
    )
    placed = dot(stacked.astype(BF16), order)
    row = rows_of((8, 1024))
    owner = jnp.broadcast_to(owner_order[...].reshape(1, 640), (8, 640))
    owner = jnp.concatenate([owner, jnp.zeros((8, 384), jnp.int32)], axis=1)
    values = (placed[:8] * 8.0 + placed[8:]).astype(jnp.int32) - 1
    columns[...] = jnp.where(row == 0, values, owner)


def start_kernel(
    live, send_order, owner_order, right, first, second, third, lower, link, mine, theirs, wide,
    masks, columns, lower_out, link_out, live_buffer, send_buffer, owner_buffer, right_buffer,
    first_buffer, second_buffer, third_buffer, semaphores,
):
    buffers = (
        live_buffer, send_buffer, owner_buffer, right_buffer, first_buffer, second_buffer,
        third_buffer, lower_out, link_out,
    )
    sources = (live, send_order, owner_order, right, first, second, third, lower, link)
    copies = fetch(sources, buffers, semaphores)
    for copy in copies[:7]:
        copy.wait()
    lane = lanes((1, 1024))
    turn = lane & 7
    wanted = (((lane >> 3) & 15) * 8 + (lane >> 7)) * 5 + turn
    order = one_hot(rows_of((640, 1024)) == jnp.where(turn < 5, wanted, -1))
    pick_rows(send_buffer, owner_buffer, right_buffer, order, mine, theirs)
    make_tables(
        live_buffer, send_buffer, owner_buffer, first_buffer, second_buffer, third_buffer, order,
        wide, masks, columns,
    )
    for copy in copies[7:]:
        copy.wait()


def stack_blocks(piece, count):
    block = lanes(piece.shape) // BLOCK
    zero = jnp.zeros_like(piece)
    return jnp.concatenate(
        [jnp.where(block == index, piece, zero) for index in range(count)], axis=0
    ).astype(BF16)


def masked_sum(product, rows):
    total = None
    for index, row in enumerate(rows):
        part = product[index * HALF : (index + 1) * HALF] * row
        total = part if total is None else total + part
    return total


def store_columns(out, value):
    width = out.shape[2]
    value = value.astype(BF16)
    for index in range(out.shape[0]):
        out[index] = value[:, index * width : (index + 1) * width]


def down_product(level, pieces, links, patterns, out):
    total = None
    for piece, link, pattern in zip(pieces, links, patterns):
        rows = pattern_rows(pattern, level)
        stack = stack_blocks(piece, len(rows))
        product = dot(stack, link[...]) if level == 1 else dot_turned(stack, link[...])
        part = masked_sum(product, rows)
        total = part if total is None else total + part
    store_columns(out, total)


def apply_factor(full, factor):
    if factor.shape[0] < full.shape[1]:
        return dot_turned(full, factor[...])
    return dot(full, factor[...])


def back_product(level, full, link, pattern):
    rows = pattern_rows(pattern, level)
    stacked = jnp.concatenate([full * row for row in rows], axis=0).astype(BF16)
    product = apply_factor(stacked, link)
    block = lanes((HALF, product.shape[1])) // BLOCK
    total = product[:HALF]
    for index in range(1, len(rows)):
        part = product[index * HALF : (index + 1) * HALF]
        total = jnp.where(block == index, part, total)
    return total


def store_copies(out, value):
    value = value.astype(BF16)
    for index in range(out.shape[0]):
        out[index] = value


def joined(gathered):
    return jnp.concatenate([gathered[index] for index in range(gathered.shape[0])], axis=1)


def pick_rest(turned, own_columns, other_columns, outs):
    core = core_index()
    chip = lax.axis_index("x")
    parts = []
    for columns, which in ((own_columns, core), (other_columns, 1 - core)):
        source, turn = source_and_turn(columns[1:2, :640])
        hot = one_hot(rows_of((1024, 640)) == source * 8 + turn)
        start = pl.multiple_of(chip * 32 + which * HALF, HALF)
        parts.append(dot(turned[pl.ds(start, HALF), :], hot))
    offset = LEAF
    for out in outs:
        width = out.shape[1] // 2
        own, other = (part[:, offset : offset + width] for part in parts)
        out[...] = in_order(own, other).astype(BF16)
        offset += width


def in_kernel(
    received, own_pattern, other_pattern, own_lower, other_lower, own_link, other_link,
    own_columns, other_columns, own_out, other_out, first_out, second_out, third_out, out, turned,
):
    flat = received[...].reshape(1024, 128)
    turned[...] = flat.astype(F32).T.astype(BF16)
    info = received[pl.ds(lax.axis_index(LEAVES) * 4, 4)].astype(F32)
    rows = rows_of((1024, 128))
    lane = lanes((1, 128))
    fronts = []
    for chip in range(4):
        tile = info[chip]
        tails = (tile[7:8, :], tile[15:16, :])
        tail_high = jnp.where(lane < 64, tails[0], tails[1])
        tail_low = jnp.broadcast_to(jnp.where(lane < 64, tails[1], tails[0]), (8, 128))
        tail_low = pltpu.roll(tail_low, 64, 1)[0:1, :]
        positions = (
            tile[5:6, :] * 8.0 + tile[6:7, :],
            tail_high * 8.0 + tail_low,
            tile[13:14, :] * 8.0 + tile[14:15, :],
        )
        hot = jnp.concatenate(
            [one_hot(rows == position.astype(jnp.int32)) for position in positions], axis=1
        )
        picked = dot(turned[chip * 32 : (chip + 1) * 32, :], hot)
        fronts.append(
            jnp.where(lanes((HALF, 384)) < LEAF, picked[:HALF], picked[HALF:]).astype(BF16)
        )
    pick_rest(turned, own_columns, other_columns, (first_out, second_out, third_out))
    front = jnp.concatenate(fronts, axis=1)
    own = apply_factor(front, own_lower).astype(BF16)
    other = apply_factor(front, other_lower).astype(BF16)
    own_out[...] = own
    other_out[...] = other
    pieces = (own.astype(F32), other.astype(F32))
    down_product(1, pieces, (own_link, other_link), (own_pattern, other_pattern), out)


def reduce_kernel(level, received, right, masks, out):
    share = received[0].astype(F32)
    for index in range(1, received.shape[0]):
        share = share + received[index].astype(F32)
    store_copies(out, (right[...].astype(F32) - share) * chip_mask(masks, level))


def solve_pieces(level, gathered, masks, own_factor, other_factor):
    full = joined(gathered)
    own_mask, other_mask = piece_masks(masks, level)
    own = (apply_factor(full, own_factor) * own_mask).astype(BF16)
    other = (apply_factor(full, other_factor) * other_mask).astype(BF16)
    return own, other


def up_kernel(
    level, gathered, masks, own_pattern, other_pattern, own_lower, other_lower, own_link,
    other_link, own_out, other_out, out,
):
    own, other = solve_pieces(level, gathered, masks, own_lower, other_lower)
    own_out[...] = own
    other_out[...] = other
    pieces = (own.astype(F32), other.astype(F32))
    links = (own_link, other_link)
    down_product(level + 1, pieces, links, (own_pattern, other_pattern), out)


def solve_kernel(level, gathered, masks, own_factor, other_factor, own_out, other_out, out):
    own, other = solve_pieces(level, gathered, masks, own_factor, other_factor)
    own_out[...] = own
    other_out[...] = other
    store_copies(out, in_order(own.astype(F32), other.astype(F32)))


def top_kernel(level, gathered, masks, own_factor, other_factor, out):
    own, other = solve_pieces(level, gathered, masks, own_factor, other_factor)
    store_copies(out, in_order(own.astype(F32), other.astype(F32)))


def back_kernel(
    level, gathered, masks, own_pattern, other_pattern, own_y, other_y, own_link, other_link, out
):
    full = joined(gathered).astype(F32)
    own = own_y[...].astype(F32) - back_product(level + 1, full, own_link, own_pattern)
    other = other_y[...].astype(F32) - back_product(level + 1, full, other_link, other_pattern)
    if level:
        own_mask, other_mask = piece_masks(masks, level)
        own = own * own_mask
        other = other * other_mask
        store_copies(out, in_order(own, other))
    else:
        out[...] = in_order(own, other).astype(BF16)


def out_kernel(
    own_part, first_part, second_part, third_part, own_owner, other_owner, own_first, other_first,
    own_second, other_second, own_third, other_third, own_upper, other_upper, out, row,
):
    chip = lax.axis_index("x")
    core = core_index()
    for step, part in enumerate((own_part, first_part, second_part, third_part)):
        start = pl.multiple_of((chip ^ step) * (2 * LEAF), 128)
        row[:, pl.ds(start, 2 * LEAF)] = part[...]
    full = row[...]
    tails = ((own_first, own_second, own_third), (other_first, other_second, other_third))
    placed = []
    uppers = (own_upper, other_upper)
    for which, owner in enumerate((own_owner, other_owner)):
        source, turn = source_and_turn(owner[1:2, :640])
        slot = (source & 1) * 512 + (source >> 1) * 8 + turn
        hot = one_hot(rows_of((1024, 640)) == slot)
        leaf = apply_factor(full, uppers[which])
        front = jnp.concatenate([leaf] + [tail[...].astype(F32) for tail in tails[which]], axis=1)
        total = dot_turned(front.astype(BF16), hot)
        placed.append(jnp.concatenate([total[:, :512], total[:, 512:]], axis=0))
    first = jnp.where(core == 0, placed[0], placed[1])
    second = jnp.where(core == 0, placed[1], placed[0])
    unused = jnp.zeros((64, 512), F32)
    stacked = jnp.concatenate([first, second, unused], axis=0)
    out[...] = stacked.T.reshape(64, 8, 128).astype(BF16)


def final_kernel(received, far, columns, out):
    core = core_index()
    halves = []
    for ref in (received, far):
        tiles = ref[...].astype(F32).reshape(16, 4, 8, 128)
        tiles = jnp.concatenate([tiles[:, chip] for chip in range(4)], axis=0)
        turned = tiles.reshape(512, 128).T
        values = []
        for half in range(2):
            pieces = []
            for chip in range(4):
                for part in range(2):
                    start = (2 * part + half) * HALF
                    pieces.append(
                        turned[start : start + HALF, chip * 128 : (chip + 1) * 128]
                    )
            values.append(jnp.concatenate(pieces, axis=1))
        halves.append(jnp.where(core == 0, values[0], values[1]))
    top = jnp.where(core == 0, halves[0], halves[1])
    bottom = jnp.where(core == 0, halves[1], halves[0])
    value = jnp.concatenate([top, bottom], axis=0).astype(BF16)
    hot = one_hot(rows_of((640, 1024)) == columns[0:1, :])
    out[...] = dot_turned(value, hot).astype(BF16)


def per_device(
    right_side,
    send_order,
    owner_order,
    live_rows,
    lower_leaf,
    upper_leaf,
    lower_first,
    lower_second,
    lower_third,
    upper_first,
    upper_second,
    upper_third,
    downlink_first,
    downlink_second,
    downlink_third,
    uplink_first,
    uplink_second,
    uplink_third,
    pattern_first,
    pattern_second,
    pattern_third,
):
    factors = {
        "lower1": lower_first,
        "down2": downlink_second,
        "lower2": lower_second,
        "down3": downlink_third,
        "lower3": lower_third.T,
        "upper3": upper_third.T,
        "back3": uplink_third,
        "upper2": upper_second,
        "back2": uplink_second,
        "upper1": upper_first,
        "back1": uplink_first.T,
        "upper0": upper_leaf.T,
    }
    pairs = {}

    def begin(value, names):
        tied = lax.optimization_barrier((value,) + tuple(factors[name] for name in names))
        for name, factor in zip(names, tied[1:]):
            pairs[name] = (factors[name], swap(factor))
        return tied[0]

    def finish(value, names):
        tied = lax.optimization_barrier((value,) + tuple(pairs[name][1] for name in names))
        for name, other in zip(names, tied[1:]):
            pairs[name] = (pairs[name][0], other)
        return tied[0]

    mine, theirs, own_patterns, masks, own_columns, own_lower, own_link = call(
        start_kernel,
        "start",
        [
            ((16, 8, 128), BF16),
            ((16, 8, 128), BF16),
            ((16, SEP), BF16),
            ((8, 896), F32),
            ((8, 1024), jnp.int32),
            ((LEAF, 8 * LEAF), BF16),
            ((LEAF, SEP), BF16),
        ],
        (),
        distant=(
            live_rows,
            send_order,
            owner_order,
            right_side,
            pattern_first.T,
            pattern_second.T,
            pattern_third.T,
            lower_leaf.T,
            downlink_first.T,
        ),
        scratch=[
            pltpu.SMEM((14,), jnp.int32),
            pltpu.VMEM((640,), jnp.int32),
            pltpu.VMEM((640,), jnp.int32),
            pltpu.VMEM((32, 640), BF16),
            pltpu.VMEM((3, BLOCK), jnp.int32),
            pltpu.VMEM((4, BLOCK), jnp.int32),
            pltpu.VMEM((2, BLOCK), jnp.int32),
        ],
    )
    factors["lower0"] = own_lower
    factors["down1"] = own_link
    other_columns = swap(own_columns)
    other_patterns = swap(own_patterns)
    payload = call(
        pack_kernel, "pack_rows", [((16, 4, 16, 128), BF16)], (mine, swap(theirs))
    )[0]
    payload, other_columns, other_patterns = lax.optimization_barrier(
        (payload, other_columns, other_patterns)
    )
    patterns = (own_patterns, other_patterns)
    payload = begin(payload, FIRST)
    received = finish(exchange(payload.reshape(64, 16, 128), 4), FIRST)
    own_y, other_y, *rights, term = call(
        in_kernel,
        "leaf_front",
        [
            ((HALF, LEAF), BF16),
            ((HALF, LEAF), BF16),
            ((HALF, 512), BF16),
            ((HALF, 256), BF16),
            ((HALF, 128), BF16),
            ((8, HALF, 512), BF16),
        ],
        (received,)
        + patterns
        + pairs["lower0"]
        + pairs["down1"]
        + (own_columns, other_columns),
        scratch=[pltpu.VMEM((128, 1024), BF16)],
    )
    level_y = {0: (own_y, other_y)}
    for level in (1, 2, 3):
        members = MEMBERS[level]
        chip_width = SEP // members
        piece = ((HALF, WIDTHS[level]), BF16)
        if level == 1:
            term = begin(term, SECOND)
        shared = exchange(term, level)
        reduced = call(
            functools.partial(reduce_kernel, level),
            "reduce_%d" % level,
            [((members, HALF, chip_width), BF16)],
            (shared, rights[level - 1], masks),
        )[0]
        if level == 1:
            reduced = begin(finish(reduced, SECOND), THIRD)
        elif level == 2:
            reduced = begin(finish(reduced, THIRD), FOURTH)
        else:
            reduced = finish(reduced, FOURTH)
        gathered = exchange(reduced, level)
        if level < 3:
            above = MEMBERS[level + 1]
            own_y, other_y, term = call(
                functools.partial(up_kernel, level),
                "up_%d" % level,
                [piece, piece, ((above, HALF, SEP // above), BF16)],
                (gathered, masks)
                + patterns
                + pairs["lower%d" % level]
                + pairs["down%d" % (level + 1)],
            )
        else:
            copies = call(
                functools.partial(top_kernel, level),
                "top_lower",
                [((members, HALF, chip_width), BF16)],
                (gathered, masks) + pairs["lower3"],
            )[0]
            break
        level_y[level] = (own_y, other_y)
    level_x = {}
    for level in (3, 2, 1):
        members = MEMBERS[level]
        chip_width = SEP // members
        piece = ((HALF, WIDTHS[level]), BF16)
        gathered = exchange(copies, level)
        own_x, other_x, copies = call(
            functools.partial(solve_kernel, level),
            "solve_%d" % level,
            [piece, piece, ((members, HALF, chip_width), BF16)],
            (gathered, masks) + pairs["upper%d" % level],
        )
        level_x[level] = (own_x, other_x)
        gathered = exchange(copies, level)
        below = level - 1
        shape = (HALF, 2 * WIDTHS[below])
        copies = call(
            functools.partial(back_kernel, below),
            "back_%d" % below,
            [((MEMBERS[below],) + shape if below else shape, BF16)],
            (gathered, masks) + patterns + level_y[below] + pairs["back%d" % level],
        )[0]
    parts = [copies]
    for step in (1, 2, 3):
        ring = [(source, source ^ step) for source in range(4)]
        parts.append(lax.ppermute(copies, "x", ring))
    outbound = call(
        out_kernel,
        "leaf_solution",
        [((64, 8, 128), BF16)],
        tuple(parts)
        + (own_columns, other_columns)
        + level_x[1]
        + level_x[2]
        + level_x[3]
        + pairs["upper0"],
        scratch=[pltpu.VMEM((HALF, 8 * LEAF), BF16)],
    )[0]
    returned = exchange(outbound, 4)
    return call(
        final_kernel,
        "natural_order",
        [((2 * HALF, 640), BF16)],
        (returned, swap(returned), own_columns),
    )[0]


def solution(mesh):
    fine = Mesh(mesh.devices.reshape(2, 2, 2, 2, 4, 2), EVERY)
    by_column = P(None, EVERY)
    placed = (by_column, P(EVERY), P(EVERY), P()) + (by_column,) * 17
    return jax.shard_map(
        per_device, mesh=fine, in_specs=placed, out_specs=by_column, check_vma=False
    )
```

```python
import functools

import jax
import jax.numpy as jnp
from jax import lax
from jax.experimental import pallas as pl
from jax.experimental.pallas import tpu as pltpu
from jax.sharding import Mesh, PartitionSpec as P

EVERY = ("z1", "z0", "y1", "y0", "x", "c")
LEAVES = ("z1", "z0", "y1", "y0")
CHIPS = {
    0: ("x",),
    1: ("y0", "x"),
    2: ("y1", "y0", "x"),
    3: ("z0", "y1", "y0", "x"),
    4: ("z1", "z0", "y1", "y0", "x"),
}
MEMBERS = {0: 4, 1: 8, 2: 16, 3: 32, 4: 64}
FIRST = ("leaf", "lower1", "down2")
SECOND = ("second",)
THIRD = ("third", "back2")
FOURTH = ("middle", "upper1", "last")
LEAF_ROWS = 1536
HALF = 16
SEP = 4096
BLOCK = 64
LEAF = 192
WIDTHS = {0: 192, 1: 256, 2: 128, 3: 64}
FIRST_NODE = {1: 0, 2: 8, 3: 12}
F32 = jnp.float32
BF16 = jnp.bfloat16
VMEM_SPEC = pl.BlockSpec(memory_space=pltpu.VMEM)
HBM_SPEC = pl.BlockSpec(memory_space=pltpu.HBM)


def swap(value):
    return lax.ppermute(value, "c", [(0, 1), (1, 0)])


def exchange(value, level):
    return lax.all_to_all(value, CHIPS[level], split_axis=0, concat_axis=0, tiled=True)


def call(body, name, outs, operands, distant=(), scratch=()):
    constrained = [pltpu.with_memory_space_constraint(value, pltpu.HBM) for value in distant]
    scratch = list(scratch)
    if distant:
        scratch.append(pltpu.SemaphoreType.DMA((len(distant),)))
    return pl.pallas_call(
        body,
        name=name,
        out_shape=[jax.ShapeDtypeStruct(shape, dtype) for shape, dtype in outs],
        in_specs=[HBM_SPEC] * len(distant) + [VMEM_SPEC] * len(operands),
        out_specs=[VMEM_SPEC] * len(outs),
        scratch_shapes=scratch,
        compiler_params=pltpu.CompilerParams(vmem_limit_bytes=12 * 1024 * 1024),
    )(*constrained, *operands)


def fetch(sources, buffers, semaphores):
    copies = [
        pltpu.make_async_copy(source, buffer, semaphores.at[index])
        for index, (source, buffer) in enumerate(zip(sources, buffers))
    ]
    for copy in copies:
        copy.start()
    return copies


def windowed(body, place, *windows):
    def run(*refs):
        pair = refs[place : place + 2]
        pieces = [ref.at[window] for window in windows for ref in pair]
        body(*refs[:place], *pieces, *refs[place + 2 :])

    return run


def fetching(body, sources, leading, targets):
    def run(*refs):
        rest = refs[sources:]
        extra = len({place for place, _ in targets})
        joint = rest[leading : leading + extra]
        goals = [joint[place].at[window] for place, window in targets]
        copies = fetch(refs[:sources], goals, refs[-1])
        body(*rest[:leading], *rest[leading + extra : -1])
        for copy in copies:
            copy.wait()

    return run


LEFT = (slice(None), slice(0, 128))
RIGHT = (slice(None), slice(128, 256))
UPPER = (slice(0, 64), slice(None))
LOWER = (slice(64, 128), slice(None))
LEAF_LEFT = (slice(None), slice(0, LEAF_ROWS))
LEAF_RIGHT = (slice(None), slice(LEAF_ROWS, LEAF_ROWS + SEP))


def dot(left, right):
    return jnp.dot(left, right, preferred_element_type=F32)


def lanes(shape):
    return lax.broadcasted_iota(jnp.int32, shape, len(shape) - 1)


def rows_of(shape):
    return lax.broadcasted_iota(jnp.int32, shape, 0)


def one_hot(matches):
    return jnp.where(matches, 1.0, 0.0).astype(BF16)


def dot_turned(left, right):
    return lax.dot_general(left, right, (((1,), (1,)), ((), ())), preferred_element_type=F32)


def core_index():
    return lax.axis_index("c")


def source_and_turn(order):
    source = (order * 6554) >> 15
    return source, order - source * 5


def in_order(own, other):
    core = core_index()
    first = jnp.where(core == 0, own, other)
    second = jnp.where(core == 0, other, own)
    return jnp.concatenate([first, second], axis=1)


def chip_mask(masks, level):
    start = {1: 0, 2: 512, 3: 768}[level]
    return masks[0:1, start : start + 2 * WIDTHS[level]]


def piece_masks(masks, level):
    width = WIDTHS[level]
    whole = chip_mask(masks, level)
    core = core_index()
    first = whole[:, :width]
    second = whole[:, width:]
    return jnp.where(core == 0, first, second), jnp.where(core == 0, second, first)


def pattern_rows(patterns, level):
    start = {1: 0, 2: 3, 3: 7}[level]
    count = {1: 3, 2: 4, 3: 2}[level]
    return [patterns[start + row : start + row + 1, :].astype(F32) for row in range(count)]


def pick_rows(send_order, owner_order, right, order, mine, theirs):
    core = core_index()
    send = send_order[...].reshape(1, 640)
    owner = owner_order[...].reshape(1, 640)
    natural = dot(right[...], one_hot(rows_of((640, 640)) == send)).astype(BF16)
    picked = dot(natural, order)
    source, turn = source_and_turn(owner)
    high = jnp.broadcast_to(source[:, :256].astype(F32), (8, 256))
    low = jnp.broadcast_to(turn[:, :256].astype(F32), (8, 256))
    high_left = pltpu.roll(high, 192, 1)[:, :128]
    low_left = pltpu.roll(low, 192, 1)[:, :128]
    high_right = pltpu.roll(high, 64, 1)[:, :128]
    main_high = jnp.where(core == 0, high[:, :128], high_left)
    main_low = jnp.where(core == 0, low[:, :128], low_left)
    lane = lanes((8, 128))
    tail = jnp.where(
        core == 0,
        jnp.where(lane < 64, high[:, 128:], low_left),
        jnp.where(lane < 64, low[:, :128], high_right),
    )
    row = rows_of((8, 128))
    info = jnp.where(row == 5, main_high, 0.0)
    info = jnp.where(row == 6, main_low, info)
    info = jnp.where(row == 7, tail, info)
    tiles = []
    for half in range(2):
        part = picked[half * HALF : (half + 1) * HALF]
        stacked = jnp.concatenate([part[:, f * 128 : (f + 1) * 128] for f in range(8)], axis=0)
        tiles.append(stacked.T.reshape(16, 8, 128) + info[None])
    mine[...] = jnp.where(core == 0, tiles[0], tiles[1]).astype(BF16)
    theirs[...] = jnp.where(core == 0, tiles[1], tiles[0]).astype(BF16)


def pack_kernel(mine, other, out):
    core = core_index()
    own = mine[...].astype(F32)
    far = other[...].astype(F32)
    first = jnp.where(core == 0, own, far)
    second = jnp.where(core == 0, far, own)
    tiles = jnp.concatenate([first, second], axis=1).astype(BF16)
    for copy in range(4):
        out[:, copy] = tiles


def make_tables(
    live, send_order, owner_order, first, second, third, order, wide, masks, columns
):
    hot = one_hot(lanes((BLOCK, SEP)) // BLOCK == rows_of((BLOCK, SEP)))
    start = 0
    wide[...] = jnp.zeros_like(wide)
    for pattern in (first, second, third):
        count = pattern.shape[0]
        wide[start : start + count, :] = dot(
            pattern[...].astype(F32).astype(BF16), hot
        ).astype(BF16)
        start += count
    leaf = lax.axis_index(LEAVES)
    chip = lax.axis_index("x")
    for level, start in ((1, 0), (2, 512), (3, 768)):
        width = 2 * WIDTHS[level]
        member = leaf & (2**level - 1)
        row = (member * 4 + chip) * width + lanes((8, width))
        count = live[FIRST_NODE[level] + (leaf >> level)]
        masks[:, start : start + width] = (row < count).astype(F32)
    send = send_order[...].reshape(1, 640) + 1
    stacked = jnp.concatenate(
        [
            jnp.broadcast_to(digit.astype(F32), (8, 640))
            for digit in (send >> 3, send & 7)
        ],
        axis=0,
    )
    placed = dot(stacked.astype(BF16), order)
    row = rows_of((8, 1024))
    owner = jnp.broadcast_to(owner_order[...].reshape(1, 640), (8, 640))
    owner = jnp.concatenate([owner, jnp.zeros((8, 384), jnp.int32)], axis=1)
    values = (placed[:8] * 8.0 + placed[8:]).astype(jnp.int32) - 1
    columns[...] = jnp.where(row == 0, values, owner)


def start_kernel(
    live, send_order, owner_order, right, first, second, third, lower, link, mine, theirs, wide,
    masks, columns, leaf_out, live_buffer, send_buffer, owner_buffer, right_buffer,
    first_buffer, second_buffer, third_buffer, semaphores,
):
    buffers = (
        live_buffer, send_buffer, owner_buffer, right_buffer, first_buffer, second_buffer,
        third_buffer, leaf_out.at[LEAF_LEFT], leaf_out.at[LEAF_RIGHT],
    )
    sources = (live, send_order, owner_order, right, first, second, third, lower, link)
    copies = fetch(sources, buffers, semaphores)
    for copy in copies[:7]:
        copy.wait()
    lane = lanes((1, 1024))
    turn = lane & 7
    wanted = (((lane >> 3) & 15) * 8 + (lane >> 7)) * 5 + turn
    order = one_hot(rows_of((640, 1024)) == jnp.where(turn < 5, wanted, -1))
    pick_rows(send_buffer, owner_buffer, right_buffer, order, mine, theirs)
    make_tables(
        live_buffer, send_buffer, owner_buffer, first_buffer, second_buffer, third_buffer, order,
        wide, masks, columns,
    )
    for copy in copies[7:]:
        copy.wait()


def stack_blocks(piece, count):
    block = lanes(piece.shape) // BLOCK
    zero = jnp.zeros_like(piece)
    return jnp.concatenate(
        [jnp.where(block == index, piece, zero) for index in range(count)], axis=0
    ).astype(BF16)


def masked_sum(product, rows):
    total = None
    for index, row in enumerate(rows):
        part = product[index * HALF : (index + 1) * HALF] * row
        total = part if total is None else total + part
    return total


def store_columns(out, value):
    width = out.shape[2]
    value = value.astype(BF16)
    for index in range(out.shape[0]):
        out[index] = value[:, index * width : (index + 1) * width]


def down_product(level, pieces, links, patterns, out):
    total = None
    for piece, link, pattern in zip(pieces, links, patterns):
        rows = pattern_rows(pattern, level)
        stack = stack_blocks(piece, len(rows))
        product = dot(stack, link[...]) if level == 1 else dot_turned(stack, link[...])
        part = masked_sum(product, rows)
        total = part if total is None else total + part
    store_columns(out, total)


def apply_factor(full, factor):
    if factor.shape[0] < full.shape[1]:
        return dot_turned(full, factor[...])
    return dot(full, factor[...])


def back_product(level, full, link, pattern):
    rows = pattern_rows(pattern, level)
    stacked = jnp.concatenate([full * row for row in rows], axis=0).astype(BF16)
    product = apply_factor(stacked, link)
    block = lanes((HALF, product.shape[1])) // BLOCK
    total = product[:HALF]
    for index in range(1, len(rows)):
        part = product[index * HALF : (index + 1) * HALF]
        total = jnp.where(block == index, part, total)
    return total


def store_copies(out, value):
    value = value.astype(BF16)
    for index in range(out.shape[0]):
        out[index] = value


def joined(gathered):
    return jnp.concatenate([gathered[index] for index in range(gathered.shape[0])], axis=1)


def pick_rest(turned, own_columns, other_columns, outs):
    core = core_index()
    chip = lax.axis_index("x")
    parts = []
    for columns, which in ((own_columns, core), (other_columns, 1 - core)):
        source, turn = source_and_turn(columns[1:2, :640])
        hot = one_hot(rows_of((1024, 640)) == source * 8 + turn)
        start = pl.multiple_of(chip * 32 + which * HALF, HALF)
        parts.append(dot(turned[pl.ds(start, HALF), :], hot))
    offset = LEAF
    for out in outs:
        width = out.shape[1] // 2
        own, other = (part[:, offset : offset + width] for part in parts)
        out[...] = in_order(own, other).astype(BF16)
        offset += width


def in_kernel(
    received, own_pattern, other_pattern, own_lower, other_lower, own_link, other_link,
    own_columns, other_columns, own_out, other_out, first_out, second_out, third_out, out, turned,
):
    flat = received[...].reshape(1024, 128)
    turned[...] = flat.astype(F32).T.astype(BF16)
    info = received[pl.ds(lax.axis_index(LEAVES) * 4, 4)].astype(F32)
    rows = rows_of((1024, 128))
    lane = lanes((1, 128))
    fronts = []
    for chip in range(4):
        tile = info[chip]
        tails = (tile[7:8, :], tile[15:16, :])
        tail_high = jnp.where(lane < 64, tails[0], tails[1])
        tail_low = jnp.broadcast_to(jnp.where(lane < 64, tails[1], tails[0]), (8, 128))
        tail_low = pltpu.roll(tail_low, 64, 1)[0:1, :]
        positions = (
            tile[5:6, :] * 8.0 + tile[6:7, :],
            tail_high * 8.0 + tail_low,
            tile[13:14, :] * 8.0 + tile[14:15, :],
        )
        hot = jnp.concatenate(
            [one_hot(rows == position.astype(jnp.int32)) for position in positions], axis=1
        )
        picked = dot(turned[chip * 32 : (chip + 1) * 32, :], hot)
        fronts.append(
            jnp.where(lanes((HALF, 384)) < LEAF, picked[:HALF], picked[HALF:]).astype(BF16)
        )
    pick_rest(turned, own_columns, other_columns, (first_out, second_out, third_out))
    front = jnp.concatenate(fronts, axis=1)
    own = apply_factor(front, own_lower).astype(BF16)
    other = apply_factor(front, other_lower).astype(BF16)
    own_out[...] = own
    other_out[...] = other
    pieces = (own.astype(F32), other.astype(F32))
    down_product(1, pieces, (own_link, other_link), (own_pattern, other_pattern), out)


def reduce_kernel(level, received, right, masks, out):
    share = received[0].astype(F32)
    for index in range(1, received.shape[0]):
        share = share + received[index].astype(F32)
    store_copies(out, (right[...].astype(F32) - share) * chip_mask(masks, level))


def solve_pieces(level, gathered, masks, own_factor, other_factor):
    full = joined(gathered)
    own_mask, other_mask = piece_masks(masks, level)
    own = (apply_factor(full, own_factor) * own_mask).astype(BF16)
    other = (apply_factor(full, other_factor) * other_mask).astype(BF16)
    return own, other


def up_kernel(
    level, gathered, masks, own_pattern, other_pattern, own_lower, other_lower, own_link,
    other_link, own_out, other_out, out,
):
    own, other = solve_pieces(level, gathered, masks, own_lower, other_lower)
    own_out[...] = own
    other_out[...] = other
    pieces = (own.astype(F32), other.astype(F32))
    links = (own_link, other_link)
    down_product(level + 1, pieces, links, (own_pattern, other_pattern), out)


def solve_kernel(level, gathered, masks, own_factor, other_factor, own_out, other_out, out):
    own, other = solve_pieces(level, gathered, masks, own_factor, other_factor)
    own_out[...] = own
    other_out[...] = other
    store_copies(out, in_order(own.astype(F32), other.astype(F32)))


def top_kernel(level, gathered, masks, own_factor, other_factor, out):
    own, other = solve_pieces(level, gathered, masks, own_factor, other_factor)
    store_copies(out, in_order(own.astype(F32), other.astype(F32)))


def back_kernel(
    level, gathered, masks, own_pattern, other_pattern, own_y, other_y, own_link, other_link, out
):
    full = joined(gathered).astype(F32)
    own = own_y[...].astype(F32) - back_product(level + 1, full, own_link, own_pattern)
    other = other_y[...].astype(F32) - back_product(level + 1, full, other_link, other_pattern)
    if level:
        own_mask, other_mask = piece_masks(masks, level)
        own = own * own_mask
        other = other * other_mask
        store_copies(out, in_order(own, other))
    else:
        out[...] = in_order(own, other).astype(BF16)


def out_kernel(
    own_part, first_part, second_part, third_part, own_owner, other_owner, own_first, other_first,
    own_second, other_second, own_third, other_third, own_upper, other_upper, out, row,
):
    chip = lax.axis_index("x")
    core = core_index()
    for step, part in enumerate((own_part, first_part, second_part, third_part)):
        start = pl.multiple_of((chip ^ step) * (2 * LEAF), 128)
        row[:, pl.ds(start, 2 * LEAF)] = part[...]
    full = row[...]
    tails = ((own_first, own_second, own_third), (other_first, other_second, other_third))
    placed = []
    uppers = (own_upper, other_upper)
    for which, owner in enumerate((own_owner, other_owner)):
        source, turn = source_and_turn(owner[1:2, :640])
        slot = (source & 1) * 512 + (source >> 1) * 8 + turn
        hot = one_hot(rows_of((1024, 640)) == slot)
        leaf = apply_factor(full, uppers[which])
        front = jnp.concatenate([leaf] + [tail[...].astype(F32) for tail in tails[which]], axis=1)
        total = dot_turned(front.astype(BF16), hot)
        placed.append(jnp.concatenate([total[:, :512], total[:, 512:]], axis=0))
    first = jnp.where(core == 0, placed[0], placed[1])
    second = jnp.where(core == 0, placed[1], placed[0])
    unused = jnp.zeros((64, 512), F32)
    stacked = jnp.concatenate([first, second, unused], axis=0)
    out[...] = stacked.T.reshape(64, 8, 128).astype(BF16)


def final_kernel(received, far, columns, out):
    core = core_index()
    halves = []
    for ref in (received, far):
        tiles = ref[...].astype(F32).reshape(16, 4, 8, 128)
        tiles = jnp.concatenate([tiles[:, chip] for chip in range(4)], axis=0)
        turned = tiles.reshape(512, 128).T
        values = []
        for half in range(2):
            pieces = []
            for chip in range(4):
                for part in range(2):
                    start = (2 * part + half) * HALF
                    pieces.append(
                        turned[start : start + HALF, chip * 128 : (chip + 1) * 128]
                    )
            values.append(jnp.concatenate(pieces, axis=1))
        halves.append(jnp.where(core == 0, values[0], values[1]))
    top = jnp.where(core == 0, halves[0], halves[1])
    bottom = jnp.where(core == 0, halves[1], halves[0])
    value = jnp.concatenate([top, bottom], axis=0).astype(BF16)
    hot = one_hot(rows_of((640, 1024)) == columns[0:1, :])
    out[...] = dot_turned(value, hot).astype(BF16)


def per_device(
    right_side,
    send_order,
    owner_order,
    live_rows,
    lower_leaf,
    upper_leaf,
    lower_first,
    lower_second,
    lower_third,
    upper_first,
    upper_second,
    upper_third,
    downlink_first,
    downlink_second,
    downlink_third,
    uplink_first,
    uplink_second,
    uplink_third,
    pattern_first,
    pattern_second,
    pattern_third,
):
    factors = {
        "lower1": lower_first,
        "down2": downlink_second,
        "back2": uplink_second,
        "upper1": upper_first,
    }
    pairs = {}

    def begin(value, names):
        tied = lax.optimization_barrier((value,) + tuple(factors[name] for name in names))
        for name, factor in zip(names, tied[1:]):
            pairs[name] = (factors[name], swap(factor))
        return tied[0]

    def finish(value, names):
        tied = lax.optimization_barrier((value,) + tuple(pairs[name][1] for name in names))
        for name, other in zip(names, tied[1:]):
            pairs[name] = (pairs[name][0], other)
        return tied[0]

    mine, theirs, own_patterns, masks, own_columns, own_leaf = call(
        start_kernel,
        "start",
        [
            ((16, 8, 128), BF16),
            ((16, 8, 128), BF16),
            ((16, SEP), BF16),
            ((8, 896), F32),
            ((8, 1024), jnp.int32),
            ((LEAF, LEAF_ROWS + SEP), BF16),
        ],
        (),
        distant=(
            live_rows,
            send_order,
            owner_order,
            right_side,
            pattern_first.T,
            pattern_second.T,
            pattern_third.T,
            lower_leaf.T,
            downlink_first.T,
        ),
        scratch=[
            pltpu.SMEM((14,), jnp.int32),
            pltpu.VMEM((640,), jnp.int32),
            pltpu.VMEM((640,), jnp.int32),
            pltpu.VMEM((32, 640), BF16),
            pltpu.VMEM((3, BLOCK), jnp.int32),
            pltpu.VMEM((4, BLOCK), jnp.int32),
            pltpu.VMEM((2, BLOCK), jnp.int32),
        ],
    )
    factors["leaf"] = own_leaf
    other_columns = swap(own_columns)
    other_patterns = swap(own_patterns)
    payload = call(
        pack_kernel, "pack_rows", [((16, 4, 16, 128), BF16)], (mine, swap(theirs))
    )[0]
    payload, other_columns, other_patterns = lax.optimization_barrier(
        (payload, other_columns, other_patterns)
    )
    patterns = (own_patterns, other_patterns)
    payload = begin(payload, FIRST)
    received = finish(exchange(payload.reshape(64, 16, 128), 4), FIRST)
    own_y, other_y, *rights, term, factors["second"], factors["third"] = call(
        fetching(
            windowed(in_kernel, 3, LEAF_LEFT, LEAF_RIGHT),
            4,
            13,
            ((0, LEFT), (0, RIGHT), (1, UPPER), (1, LOWER)),
        ),
        "leaf_front",
        [
            ((HALF, LEAF), BF16),
            ((HALF, LEAF), BF16),
            ((HALF, 512), BF16),
            ((HALF, 256), BF16),
            ((HALF, 128), BF16),
            ((8, HALF, 512), BF16),
            ((SEP, 256), BF16),
            ((128, SEP), BF16),
        ],
        (received,) + patterns + pairs["leaf"] + (own_columns, other_columns),
        distant=(lower_second, downlink_third, lower_third.T, upper_third.T),
        scratch=[pltpu.VMEM((128, 1024), BF16)],
    )
    level_y = {0: (own_y, other_y)}
    for level in (1, 2, 3):
        members = MEMBERS[level]
        chip_width = SEP // members
        piece = ((HALF, WIDTHS[level]), BF16)
        if level == 1:
            term = begin(term, SECOND)
        shared = exchange(term, level)
        reduced = call(
            functools.partial(reduce_kernel, level),
            "reduce_%d" % level,
            [((members, HALF, chip_width), BF16)],
            (shared, rights[level - 1], masks),
        )[0]
        if level == 1:
            reduced = begin(finish(reduced, SECOND), THIRD)
        elif level == 2:
            reduced = begin(finish(reduced, THIRD), FOURTH)
        else:
            reduced = finish(reduced, FOURTH)
        gathered = exchange(reduced, level)
        if level < 3:
            above = MEMBERS[level + 1]
            outs = [piece, piece, ((above, HALF, SEP // above), BF16)]
            operands = (gathered, masks) + patterns
            body = functools.partial(up_kernel, level)
            if level == 1:
                own_y, other_y, term, factors["middle"], factors["last"] = call(
                    fetching(body, 4, 11, ((0, LEFT), (0, RIGHT), (1, LEAF_RIGHT), (1, LEAF_LEFT))),
                    "up_1",
                    outs + [((SEP, 256), BF16), ((LEAF, LEAF_ROWS + SEP), BF16)],
                    operands + pairs["lower1"] + pairs["down2"],
                    distant=(uplink_third, upper_second, uplink_first.T, upper_leaf.T),
                )
            else:
                own_y, other_y, term = call(
                    windowed(body, 4, LEFT, RIGHT), "up_2", outs, operands + pairs["second"]
                )
        else:
            copies = call(
                windowed(functools.partial(top_kernel, level), 2, UPPER),
                "top_lower",
                [((members, HALF, chip_width), BF16)],
                (gathered, masks) + pairs["third"],
            )[0]
            break
        level_y[level] = (own_y, other_y)
    level_x = {}
    whole = (slice(None), slice(None))
    uppers = {3: ("third", LOWER), 2: ("middle", RIGHT), 1: ("upper1", whole)}
    backs = {3: ("middle", LEFT), 2: ("back2", whole), 1: ("last", LEAF_RIGHT)}
    for level in (3, 2, 1):
        members = MEMBERS[level]
        chip_width = SEP // members
        piece = ((HALF, WIDTHS[level]), BF16)
        gathered = exchange(copies, level)
        own_x, other_x, copies = call(
            windowed(functools.partial(solve_kernel, level), 2, uppers[level][1]),
            "solve_%d" % level,
            [piece, piece, ((members, HALF, chip_width), BF16)],
            (gathered, masks) + pairs[uppers[level][0]],
        )
        level_x[level] = (own_x, other_x)
        gathered = exchange(copies, level)
        below = level - 1
        shape = (HALF, 2 * WIDTHS[below])
        copies = call(
            windowed(functools.partial(back_kernel, below), 6, backs[level][1]),
            "back_%d" % below,
            [((MEMBERS[below],) + shape if below else shape, BF16)],
            (gathered, masks) + patterns + level_y[below] + pairs[backs[level][0]],
        )[0]
    parts = [copies]
    for step in (1, 2, 3):
        ring = [(source, source ^ step) for source in range(4)]
        parts.append(lax.ppermute(copies, "x", ring))
    outbound = call(
        windowed(out_kernel, 12, LEAF_LEFT),
        "leaf_solution",
        [((64, 8, 128), BF16)],
        tuple(parts)
        + (own_columns, other_columns)
        + level_x[1]
        + level_x[2]
        + level_x[3]
        + pairs["last"],
        scratch=[pltpu.VMEM((HALF, 8 * LEAF), BF16)],
    )[0]
    returned = exchange(outbound, 4)
    return call(
        final_kernel,
        "natural_order",
        [((2 * HALF, 640), BF16)],
        (returned, swap(returned), own_columns),
    )[0]


def solution(mesh):
    fine = Mesh(mesh.devices.reshape(2, 2, 2, 2, 4, 2), EVERY)
    by_column = P(None, EVERY)
    placed = (by_column, P(EVERY), P(EVERY), P()) + (by_column,) * 17
    return jax.shard_map(
        per_device, mesh=fine, in_specs=placed, out_specs=by_column, check_vma=False
    )
```

```python
import functools

import jax
import jax.numpy as jnp
from jax import lax
from jax.experimental import pallas as pl
from jax.experimental.pallas import tpu as pltpu
from jax.sharding import Mesh, PartitionSpec as P

EVERY = ("z1", "z0", "y1", "y0", "x", "c")
LEAVES = ("z1", "z0", "y1", "y0")
CHIPS = {
    0: ("x",),
    1: ("y0", "x"),
    2: ("y1", "y0", "x"),
    3: ("z0", "y1", "y0", "x"),
    4: ("z1", "z0", "y1", "y0", "x"),
}
MEMBERS = {0: 4, 1: 8, 2: 16, 3: 32, 4: 64}
FIRST = ("leaf", "lower1", "down2")
SECOND = ("lower2", "down3")
THIRD = ("third", "back2")
FOURTH = ("middle", "upper1", "back1", "upper0")
LEAF_ROWS = 1536
HALF = 16
SEP = 4096
BLOCK = 64
LEAF = 192
WIDTHS = {0: 192, 1: 256, 2: 128, 3: 64}
FIRST_NODE = {1: 0, 2: 8, 3: 12}
F32 = jnp.float32
BF16 = jnp.bfloat16
VMEM_SPEC = pl.BlockSpec(memory_space=pltpu.VMEM)
HBM_SPEC = pl.BlockSpec(memory_space=pltpu.HBM)


def swap(value):
    return lax.ppermute(value, "c", [(0, 1), (1, 0)])


def exchange(value, level):
    return lax.all_to_all(value, CHIPS[level], split_axis=0, concat_axis=0, tiled=True)


def call(body, name, outs, operands, distant=(), scratch=()):
    constrained = [pltpu.with_memory_space_constraint(value, pltpu.HBM) for value in distant]
    scratch = list(scratch)
    if distant:
        scratch.append(pltpu.SemaphoreType.DMA((len(distant),)))
    return pl.pallas_call(
        body,
        name=name,
        out_shape=[jax.ShapeDtypeStruct(shape, dtype) for shape, dtype in outs],
        in_specs=[HBM_SPEC] * len(distant) + [VMEM_SPEC] * len(operands),
        out_specs=[VMEM_SPEC] * len(outs),
        scratch_shapes=scratch,
        compiler_params=pltpu.CompilerParams(vmem_limit_bytes=12 * 1024 * 1024),
    )(*constrained, *operands)


def fetch(sources, buffers, semaphores):
    copies = [
        pltpu.make_async_copy(source, buffer, semaphores.at[index])
        for index, (source, buffer) in enumerate(zip(sources, buffers))
    ]
    for copy in copies:
        copy.start()
    return copies


def windowed(body, place, *windows):
    def run(*refs):
        pair = refs[place : place + 2]
        pieces = [ref.at[window] for window in windows for ref in pair]
        body(*refs[:place], *pieces, *refs[place + 2 :])

    return run


def fetching(body, sources, leading, targets):
    def run(*refs):
        rest = refs[sources:]
        extra = len({place for place, _ in targets})
        joint = rest[leading : leading + extra]
        goals = [joint[place].at[window] for place, window in targets]
        copies = fetch(refs[:sources], goals, refs[-1])
        body(*rest[:leading], *rest[leading + extra : -1])
        for copy in copies:
            copy.wait()

    return run


LEFT = (slice(None), slice(0, 128))
RIGHT = (slice(None), slice(128, 256))
UPPER = (slice(0, 64), slice(None))
LOWER = (slice(64, 128), slice(None))
LEAF_LEFT = (slice(None), slice(0, LEAF_ROWS))
LEAF_RIGHT = (slice(None), slice(LEAF_ROWS, LEAF_ROWS + SEP))


def dot(left, right):
    return jnp.dot(left, right, preferred_element_type=F32)


def lanes(shape):
    return lax.broadcasted_iota(jnp.int32, shape, len(shape) - 1)


def rows_of(shape):
    return lax.broadcasted_iota(jnp.int32, shape, 0)


def one_hot(matches):
    return jnp.where(matches, 1.0, 0.0).astype(BF16)


def dot_turned(left, right):
    return lax.dot_general(left, right, (((1,), (1,)), ((), ())), preferred_element_type=F32)


def core_index():
    return lax.axis_index("c")


def source_and_turn(order):
    source = (order * 6554) >> 15
    return source, order - source * 5


def in_order(own, other):
    core = core_index()
    first = jnp.where(core == 0, own, other)
    second = jnp.where(core == 0, other, own)
    return jnp.concatenate([first, second], axis=1)


def chip_mask(masks, level):
    start = {1: 0, 2: 512, 3: 768}[level]
    return masks[0:1, start : start + 2 * WIDTHS[level]]


def piece_masks(masks, level):
    width = WIDTHS[level]
    whole = chip_mask(masks, level)
    core = core_index()
    first = whole[:, :width]
    second = whole[:, width:]
    return jnp.where(core == 0, first, second), jnp.where(core == 0, second, first)


def pattern_rows(patterns, level):
    start = {1: 0, 2: 3, 3: 7}[level]
    count = {1: 3, 2: 4, 3: 2}[level]
    return [patterns[start + row : start + row + 1, :].astype(F32) for row in range(count)]


def pick_rows(send_order, owner_order, right, order, mine, theirs):
    core = core_index()
    send = send_order[...].reshape(1, 640)
    owner = owner_order[...].reshape(1, 640)
    natural = dot(right[...], one_hot(rows_of((640, 640)) == send)).astype(BF16)
    picked = dot(natural, order)
    source, turn = source_and_turn(owner)
    high = jnp.broadcast_to(source[:, :256].astype(F32), (8, 256))
    low = jnp.broadcast_to(turn[:, :256].astype(F32), (8, 256))
    high_left = pltpu.roll(high, 192, 1)[:, :128]
    low_left = pltpu.roll(low, 192, 1)[:, :128]
    high_right = pltpu.roll(high, 64, 1)[:, :128]
    main_high = jnp.where(core == 0, high[:, :128], high_left)
    main_low = jnp.where(core == 0, low[:, :128], low_left)
    lane = lanes((8, 128))
    tail = jnp.where(
        core == 0,
        jnp.where(lane < 64, high[:, 128:], low_left),
        jnp.where(lane < 64, low[:, :128], high_right),
    )
    row = rows_of((8, 128))
    info = jnp.where(row == 5, main_high, 0.0)
    info = jnp.where(row == 6, main_low, info)
    info = jnp.where(row == 7, tail, info)
    tiles = []
    for half in range(2):
        part = picked[half * HALF : (half + 1) * HALF]
        stacked = jnp.concatenate([part[:, f * 128 : (f + 1) * 128] for f in range(8)], axis=0)
        tiles.append(stacked.T.reshape(16, 8, 128) + info[None])
    mine[...] = jnp.where(core == 0, tiles[0], tiles[1]).astype(BF16)
    theirs[...] = jnp.where(core == 0, tiles[1], tiles[0]).astype(BF16)


def pack_kernel(mine, other, out):
    core = core_index()
    own = mine[...].astype(F32)
    far = other[...].astype(F32)
    first = jnp.where(core == 0, own, far)
    second = jnp.where(core == 0, far, own)
    tiles = jnp.concatenate([first, second], axis=1).astype(BF16)
    for copy in range(4):
        out[:, copy] = tiles


def make_tables(
    live, send_order, owner_order, first, second, third, order, wide, masks, columns
):
    hot = one_hot(lanes((BLOCK, SEP)) // BLOCK == rows_of((BLOCK, SEP)))
    start = 0
    wide[...] = jnp.zeros_like(wide)
    for pattern in (first, second, third):
        count = pattern.shape[0]
        wide[start : start + count, :] = dot(
            pattern[...].astype(F32).astype(BF16), hot
        ).astype(BF16)
        start += count
    leaf = lax.axis_index(LEAVES)
    chip = lax.axis_index("x")
    for level, start in ((1, 0), (2, 512), (3, 768)):
        width = 2 * WIDTHS[level]
        member = leaf & (2**level - 1)
        row = (member * 4 + chip) * width + lanes((8, width))
        count = live[FIRST_NODE[level] + (leaf >> level)]
        masks[:, start : start + width] = (row < count).astype(F32)
    send = send_order[...].reshape(1, 640) + 1
    stacked = jnp.concatenate(
        [
            jnp.broadcast_to(digit.astype(F32), (8, 640))
            for digit in (send >> 3, send & 7)
        ],
        axis=0,
    )
    placed = dot(stacked.astype(BF16), order)
    row = rows_of((8, 1024))
    owner = jnp.broadcast_to(owner_order[...].reshape(1, 640), (8, 640))
    owner = jnp.concatenate([owner, jnp.zeros((8, 384), jnp.int32)], axis=1)
    values = (placed[:8] * 8.0 + placed[8:]).astype(jnp.int32) - 1
    columns[...] = jnp.where(row == 0, values, owner)


def start_kernel(
    live, send_order, owner_order, right, first, second, third, lower, link, mine, theirs, wide,
    masks, columns, leaf_out, live_buffer, send_buffer, owner_buffer, right_buffer,
    first_buffer, second_buffer, third_buffer, semaphores,
):
    buffers = (
        live_buffer, send_buffer, owner_buffer, right_buffer, first_buffer, second_buffer,
        third_buffer, leaf_out.at[LEAF_LEFT], leaf_out.at[LEAF_RIGHT],
    )
    sources = (live, send_order, owner_order, right, first, second, third, lower, link)
    copies = fetch(sources, buffers, semaphores)
    for copy in copies[:7]:
        copy.wait()
    lane = lanes((1, 1024))
    turn = lane & 7
    wanted = (((lane >> 3) & 15) * 8 + (lane >> 7)) * 5 + turn
    order = one_hot(rows_of((640, 1024)) == jnp.where(turn < 5, wanted, -1))
    pick_rows(send_buffer, owner_buffer, right_buffer, order, mine, theirs)
    make_tables(
        live_buffer, send_buffer, owner_buffer, first_buffer, second_buffer, third_buffer, order,
        wide, masks, columns,
    )
    for copy in copies[7:]:
        copy.wait()


def stack_blocks(piece, count):
    block = lanes(piece.shape) // BLOCK
    zero = jnp.zeros_like(piece)
    return jnp.concatenate(
        [jnp.where(block == index, piece, zero) for index in range(count)], axis=0
    ).astype(BF16)


def masked_sum(product, rows):
    total = None
    for index, row in enumerate(rows):
        part = product[index * HALF : (index + 1) * HALF] * row
        total = part if total is None else total + part
    return total


def store_columns(out, value):
    width = out.shape[2]
    value = value.astype(BF16)
    for index in range(out.shape[0]):
        out[index] = value[:, index * width : (index + 1) * width]


def down_product(level, pieces, links, patterns, out):
    total = None
    for piece, link, pattern in zip(pieces, links, patterns):
        rows = pattern_rows(pattern, level)
        stack = stack_blocks(piece, len(rows))
        product = dot(stack, link[...]) if level == 1 else dot_turned(stack, link[...])
        part = masked_sum(product, rows)
        total = part if total is None else total + part
    store_columns(out, total)


def apply_factor(full, factor):
    if factor.shape[0] < full.shape[1]:
        return dot_turned(full, factor[...])
    return dot(full, factor[...])


def back_product(level, full, link, pattern):
    rows = pattern_rows(pattern, level)
    stacked = jnp.concatenate([full * row for row in rows], axis=0).astype(BF16)
    product = apply_factor(stacked, link)
    block = lanes((HALF, product.shape[1])) // BLOCK
    total = product[:HALF]
    for index in range(1, len(rows)):
        part = product[index * HALF : (index + 1) * HALF]
        total = jnp.where(block == index, part, total)
    return total


def store_copies(out, value):
    value = value.astype(BF16)
    for index in range(out.shape[0]):
        out[index] = value


def joined(gathered):
    return jnp.concatenate([gathered[index] for index in range(gathered.shape[0])], axis=1)


def pick_rest(turned, own_columns, other_columns, outs):
    core = core_index()
    chip = lax.axis_index("x")
    parts = []
    for columns, which in ((own_columns, core), (other_columns, 1 - core)):
        source, turn = source_and_turn(columns[1:2, :640])
        hot = one_hot(rows_of((1024, 640)) == source * 8 + turn)
        start = pl.multiple_of(chip * 32 + which * HALF, HALF)
        parts.append(dot(turned[pl.ds(start, HALF), :], hot))
    offset = LEAF
    for out in outs:
        width = out.shape[1] // 2
        own, other = (part[:, offset : offset + width] for part in parts)
        out[...] = in_order(own, other).astype(BF16)
        offset += width


def in_kernel(
    received, own_pattern, other_pattern, own_lower, other_lower, own_link, other_link,
    own_columns, other_columns, own_out, other_out, first_out, second_out, third_out, out, turned,
):
    flat = received[...].reshape(1024, 128)
    turned[...] = flat.astype(F32).T.astype(BF16)
    info = received[pl.ds(lax.axis_index(LEAVES) * 4, 4)].astype(F32)
    rows = rows_of((1024, 128))
    lane = lanes((1, 128))
    fronts = []
    for chip in range(4):
        tile = info[chip]
        tails = (tile[7:8, :], tile[15:16, :])
        tail_high = jnp.where(lane < 64, tails[0], tails[1])
        tail_low = jnp.broadcast_to(jnp.where(lane < 64, tails[1], tails[0]), (8, 128))
        tail_low = pltpu.roll(tail_low, 64, 1)[0:1, :]
        positions = (
            tile[5:6, :] * 8.0 + tile[6:7, :],
            tail_high * 8.0 + tail_low,
            tile[13:14, :] * 8.0 + tile[14:15, :],
        )
        hot = jnp.concatenate(
            [one_hot(rows == position.astype(jnp.int32)) for position in positions], axis=1
        )
        picked = dot(turned[chip * 32 : (chip + 1) * 32, :], hot)
        fronts.append(
            jnp.where(lanes((HALF, 384)) < LEAF, picked[:HALF], picked[HALF:]).astype(BF16)
        )
    pick_rest(turned, own_columns, other_columns, (first_out, second_out, third_out))
    front = jnp.concatenate(fronts, axis=1)
    own = apply_factor(front, own_lower).astype(BF16)
    other = apply_factor(front, other_lower).astype(BF16)
    own_out[...] = own
    other_out[...] = other
    pieces = (own.astype(F32), other.astype(F32))
    down_product(1, pieces, (own_link, other_link), (own_pattern, other_pattern), out)


def reduce_kernel(level, received, right, masks, out):
    share = received[0].astype(F32)
    for index in range(1, received.shape[0]):
        share = share + received[index].astype(F32)
    store_copies(out, (right[...].astype(F32) - share) * chip_mask(masks, level))


def solve_pieces(level, gathered, masks, own_factor, other_factor):
    full = joined(gathered)
    own_mask, other_mask = piece_masks(masks, level)
    own = (apply_factor(full, own_factor) * own_mask).astype(BF16)
    other = (apply_factor(full, other_factor) * other_mask).astype(BF16)
    return own, other


def up_kernel(
    level, gathered, masks, own_pattern, other_pattern, own_lower, other_lower, own_link,
    other_link, own_out, other_out, out,
):
    own, other = solve_pieces(level, gathered, masks, own_lower, other_lower)
    own_out[...] = own
    other_out[...] = other
    pieces = (own.astype(F32), other.astype(F32))
    links = (own_link, other_link)
    down_product(level + 1, pieces, links, (own_pattern, other_pattern), out)


def solve_kernel(level, gathered, masks, own_factor, other_factor, own_out, other_out, out):
    own, other = solve_pieces(level, gathered, masks, own_factor, other_factor)
    own_out[...] = own
    other_out[...] = other
    store_copies(out, in_order(own.astype(F32), other.astype(F32)))


def top_kernel(level, gathered, masks, own_factor, other_factor, out):
    own, other = solve_pieces(level, gathered, masks, own_factor, other_factor)
    store_copies(out, in_order(own.astype(F32), other.astype(F32)))


def back_kernel(
    level, gathered, masks, own_pattern, other_pattern, own_y, other_y, own_link, other_link, out
):
    full = joined(gathered).astype(F32)
    own = own_y[...].astype(F32) - back_product(level + 1, full, own_link, own_pattern)
    other = other_y[...].astype(F32) - back_product(level + 1, full, other_link, other_pattern)
    if level:
        own_mask, other_mask = piece_masks(masks, level)
        own = own * own_mask
        other = other * other_mask
        store_copies(out, in_order(own, other))
    else:
        out[...] = in_order(own, other).astype(BF16)


def out_kernel(
    own_part, first_part, second_part, third_part, own_owner, other_owner, own_first, other_first,
    own_second, other_second, own_third, other_third, own_upper, other_upper, out, row,
):
    chip = lax.axis_index("x")
    core = core_index()
    for step, part in enumerate((own_part, first_part, second_part, third_part)):
        start = pl.multiple_of((chip ^ step) * (2 * LEAF), 128)
        row[:, pl.ds(start, 2 * LEAF)] = part[...]
    full = row[...]
    tails = ((own_first, own_second, own_third), (other_first, other_second, other_third))
    placed = []
    uppers = (own_upper, other_upper)
    for which, owner in enumerate((own_owner, other_owner)):
        source, turn = source_and_turn(owner[1:2, :640])
        slot = (source & 1) * 512 + (source >> 1) * 8 + turn
        hot = one_hot(rows_of((1024, 640)) == slot)
        leaf = apply_factor(full, uppers[which])
        front = jnp.concatenate([leaf] + [tail[...].astype(F32) for tail in tails[which]], axis=1)
        total = dot_turned(front.astype(BF16), hot)
        placed.append(jnp.concatenate([total[:, :512], total[:, 512:]], axis=0))
    first = jnp.where(core == 0, placed[0], placed[1])
    second = jnp.where(core == 0, placed[1], placed[0])
    unused = jnp.zeros((64, 512), F32)
    stacked = jnp.concatenate([first, second, unused], axis=0)
    out[...] = stacked.T.reshape(64, 8, 128).astype(BF16)


def final_kernel(received, far, columns, out):
    core = core_index()
    halves = []
    for ref in (received, far):
        tiles = ref[...].astype(F32).reshape(16, 4, 8, 128)
        tiles = jnp.concatenate([tiles[:, chip] for chip in range(4)], axis=0)
        turned = tiles.reshape(512, 128).T
        values = []
        for half in range(2):
            pieces = []
            for chip in range(4):
                for part in range(2):
                    start = (2 * part + half) * HALF
                    pieces.append(
                        turned[start : start + HALF, chip * 128 : (chip + 1) * 128]
                    )
            values.append(jnp.concatenate(pieces, axis=1))
        halves.append(jnp.where(core == 0, values[0], values[1]))
    top = jnp.where(core == 0, halves[0], halves[1])
    bottom = jnp.where(core == 0, halves[1], halves[0])
    value = jnp.concatenate([top, bottom], axis=0).astype(BF16)
    hot = one_hot(rows_of((640, 1024)) == columns[0:1, :])
    out[...] = dot_turned(value, hot).astype(BF16)


def per_device(
    right_side,
    send_order,
    owner_order,
    live_rows,
    lower_leaf,
    upper_leaf,
    lower_first,
    lower_second,
    lower_third,
    upper_first,
    upper_second,
    upper_third,
    downlink_first,
    downlink_second,
    downlink_third,
    uplink_first,
    uplink_second,
    uplink_third,
    pattern_first,
    pattern_second,
    pattern_third,
):
    factors = {
        "lower1": lower_first,
        "down2": downlink_second,
        "lower2": lower_second,
        "down3": downlink_third,
        "back1": uplink_first.T,
        "upper0": upper_leaf.T,
        "back2": uplink_second,
        "upper1": upper_first,
    }
    pairs = {}

    def begin(value, names):
        tied = lax.optimization_barrier((value,) + tuple(factors[name] for name in names))
        for name, factor in zip(names, tied[1:]):
            pairs[name] = (factors[name], swap(factor))
        return tied[0]

    def finish(value, names):
        tied = lax.optimization_barrier((value,) + tuple(pairs[name][1] for name in names))
        for name, other in zip(names, tied[1:]):
            pairs[name] = (pairs[name][0], other)
        return tied[0]

    mine, theirs, own_patterns, masks, own_columns, own_leaf = call(
        start_kernel,
        "start",
        [
            ((16, 8, 128), BF16),
            ((16, 8, 128), BF16),
            ((16, SEP), BF16),
            ((8, 896), F32),
            ((8, 1024), jnp.int32),
            ((LEAF, LEAF_ROWS + SEP), BF16),
        ],
        (),
        distant=(
            live_rows,
            send_order,
            owner_order,
            right_side,
            pattern_first.T,
            pattern_second.T,
            pattern_third.T,
            lower_leaf.T,
            downlink_first.T,
        ),
        scratch=[
            pltpu.SMEM((14,), jnp.int32),
            pltpu.VMEM((640,), jnp.int32),
            pltpu.VMEM((640,), jnp.int32),
            pltpu.VMEM((32, 640), BF16),
            pltpu.VMEM((3, BLOCK), jnp.int32),
            pltpu.VMEM((4, BLOCK), jnp.int32),
            pltpu.VMEM((2, BLOCK), jnp.int32),
        ],
    )
    factors["leaf"] = own_leaf
    other_columns = swap(own_columns)
    other_patterns = swap(own_patterns)
    payload = call(
        pack_kernel, "pack_rows", [((16, 4, 16, 128), BF16)], (mine, swap(theirs))
    )[0]
    payload, other_columns, other_patterns = lax.optimization_barrier(
        (payload, other_columns, other_patterns)
    )
    patterns = (own_patterns, other_patterns)
    payload = begin(payload, FIRST)
    received = finish(exchange(payload.reshape(64, 16, 128), 4), FIRST)
    own_y, other_y, *rights, term, factors["third"] = call(
        fetching(
            windowed(in_kernel, 3, LEAF_LEFT, LEAF_RIGHT),
            2,
            13,
            ((0, UPPER), (0, LOWER)),
        ),
        "leaf_front",
        [
            ((HALF, LEAF), BF16),
            ((HALF, LEAF), BF16),
            ((HALF, 512), BF16),
            ((HALF, 256), BF16),
            ((HALF, 128), BF16),
            ((8, HALF, 512), BF16),
            ((128, SEP), BF16),
        ],
        (received,) + patterns + pairs["leaf"] + (own_columns, other_columns),
        distant=(lower_third.T, upper_third.T),
        scratch=[pltpu.VMEM((128, 1024), BF16)],
    )
    level_y = {0: (own_y, other_y)}
    for level in (1, 2, 3):
        members = MEMBERS[level]
        chip_width = SEP // members
        piece = ((HALF, WIDTHS[level]), BF16)
        if level == 1:
            term = begin(term, SECOND)
        shared = exchange(term, level)
        reduced = call(
            functools.partial(reduce_kernel, level),
            "reduce_%d" % level,
            [((members, HALF, chip_width), BF16)],
            (shared, rights[level - 1], masks),
        )[0]
        if level == 1:
            reduced = begin(finish(reduced, SECOND), THIRD)
        elif level == 2:
            reduced = begin(finish(reduced, THIRD), FOURTH)
        else:
            reduced = finish(reduced, FOURTH)
        gathered = exchange(reduced, level)
        if level < 3:
            above = MEMBERS[level + 1]
            outs = [piece, piece, ((above, HALF, SEP // above), BF16)]
            operands = (gathered, masks) + patterns
            body = functools.partial(up_kernel, level)
            if level == 1:
                own_y, other_y, term, factors["middle"] = call(
                    fetching(body, 2, 11, ((0, LEFT), (0, RIGHT))),
                    "up_1",
                    outs + [((SEP, 256), BF16)],
                    operands + pairs["lower1"] + pairs["down2"],
                    distant=(uplink_third, upper_second),
                )
            else:
                own_y, other_y, term = call(
                    body, "up_2", outs, operands + pairs["lower2"] + pairs["down3"]
                )
        else:
            copies = call(
                windowed(functools.partial(top_kernel, level), 2, UPPER),
                "top_lower",
                [((members, HALF, chip_width), BF16)],
                (gathered, masks) + pairs["third"],
            )[0]
            break
        level_y[level] = (own_y, other_y)
    level_x = {}
    whole = (slice(None), slice(None))
    uppers = {3: ("third", LOWER), 2: ("middle", RIGHT), 1: ("upper1", whole)}
    backs = {3: ("middle", LEFT), 2: ("back2", whole), 1: ("back1", whole)}
    for level in (3, 2, 1):
        members = MEMBERS[level]
        chip_width = SEP // members
        piece = ((HALF, WIDTHS[level]), BF16)
        gathered = exchange(copies, level)
        own_x, other_x, copies = call(
            windowed(functools.partial(solve_kernel, level), 2, uppers[level][1]),
            "solve_%d" % level,
            [piece, piece, ((members, HALF, chip_width), BF16)],
            (gathered, masks) + pairs[uppers[level][0]],
        )
        level_x[level] = (own_x, other_x)
        gathered = exchange(copies, level)
        below = level - 1
        shape = (HALF, 2 * WIDTHS[below])
        copies = call(
            windowed(functools.partial(back_kernel, below), 6, backs[level][1]),
            "back_%d" % below,
            [((MEMBERS[below],) + shape if below else shape, BF16)],
            (gathered, masks) + patterns + level_y[below] + pairs[backs[level][0]],
        )[0]
    parts = [copies]
    for step in (1, 2, 3):
        ring = [(source, source ^ step) for source in range(4)]
        parts.append(lax.ppermute(copies, "x", ring))
    outbound = call(
        out_kernel,
        "leaf_solution",
        [((64, 8, 128), BF16)],
        tuple(parts)
        + (own_columns, other_columns)
        + level_x[1]
        + level_x[2]
        + level_x[3]
        + pairs["upper0"],
        scratch=[pltpu.VMEM((HALF, 8 * LEAF), BF16)],
    )[0]
    returned = exchange(outbound, 4)
    return call(
        final_kernel,
        "natural_order",
        [((2 * HALF, 640), BF16)],
        (returned, swap(returned), own_columns),
    )[0]


def solution(mesh):
    fine = Mesh(mesh.devices.reshape(2, 2, 2, 2, 4, 2), EVERY)
    by_column = P(None, EVERY)
    placed = (by_column, P(EVERY), P(EVERY), P()) + (by_column,) * 17
    return jax.shard_map(
        per_device, mesh=fine, in_specs=placed, out_specs=by_column, check_vma=False
    )
```
